256 devices in a mesh: row: 32 (over z, y_lo, core), col: 8 (over y_hi, x).
Axes of the slice: x: 4, y: 4 (y_hi: 2, y_lo: 2; y = y_hi * 2 + y_lo), z: 8, core: 2. Of those that a mesh axis runs over, the one named last changes fastest.
Arguments:
- matrix: float32 [14336, 14336], P('row', 'col'), may hold values from -16 to 16, as said below
- panels: float32 [2, 14336, 128], P(None, 'row'), may hold values from -0.050111484 to 0.050111484
- factors: float32 [2, 128, 128], replicated, may hold values from -1.2 to 1.6, as said below
Outputs:
- updated: float32 [14336, 14336], P('row', 'col')
The draws below stay inside these ranges and needn't reach their ends.
Inputs may be any that keep to these rules, and one draw needn't show every extreme that they name: symmetric: matrix[r, c] equals matrix[c, r]. Each factors[p] is upper triangular, with diagonal entries between 0.8 and 1.6.
All inputs are finite; a program needn't handle non-finite values.
Results may differ from the reference program's by a relative error of at most 0.0001.
Values sent between devices are 32-bit elements; how exact they have to be, the bound alone decides.
A program may use at most 64 MiB of HBM per device.

```python
import math
import jax
import jax.numpy as jnp
from jax import lax

N = 14336
B = 128
PANELS = 2


def draw_matrix(key, part):
    inner_key = jax.random.fold_in(key, 101)
    normal_key = jax.random.fold_in(inner_key, 0)
    values = jax.random.normal(normal_key, (N, N), jnp.float32)
    values = jnp.clip(values, -4.0, 4.0)
    values = (values + values.T) * 0.5
    values = values * math.sqrt(2.0)
    values = jnp.clip(values, -4.0, 4.0)
    return values


def draw_factors(key, part):
    inner_key = jax.random.fold_in(key, 202)
    upper_key, diag_key = jax.random.split(inner_key)
    upper = jnp.clip(0.2 * jax.random.normal(upper_key, (PANELS, B, B), jnp.float32), -1.2, 1.2)
    upper = jnp.triu(upper, 1)
    diagonal = jax.random.uniform(diag_key, (PANELS, B), jnp.float32, 0.8, 1.6)
    return upper + jnp.eye(B, dtype=jnp.float32)[None, :, :] * diagonal[:, None, :]


def shard_levels(key, dims, shards, low, top_value):
    loudness = 1.0
    for position, shards_of in shards:
        draws = jax.random.uniform(jax.random.fold_in(jax.random.fold_in(key, 6), position), (shards_of,), jnp.float32, low / len(shards), top_value / len(shards))
        loudness = loudness * jnp.repeat(jnp.exp(draws), dims[position] // shards_of).reshape((-1,) + (1,) * (len(dims) - 1 - position))
    return loudness


def gaussian(stream_key, shape, deviation, limit, cuts=(), held_as=jnp.bfloat16):
    result = jax.random.normal(stream_key, shape, jnp.float32) * deviation
    if len(cuts) > 0:
        result = shard_levels(stream_key, shape, cuts, -0.22, 0.18) * result
    return jnp.clip(result, min=-limit, max=limit).astype(held_as)


def setup_inputs(seed: int = 0) -> dict:
    arg_keys = jax.random.split(jax.random.key(seed), 4)
    return {
        "matrix": draw_matrix(jax.random.fold_in(arg_keys[3], 71), 0),
        "panels": gaussian(arg_keys[1], (PANELS, N, B), (N ** -0.5), 0.050111484, ((1, 32),), jnp.float32),
        "factors": draw_factors(jax.random.fold_in(arg_keys[3], 71), 0),
    }


def reference(matrix, panels, factors):
    current = matrix
    for number in range(PANELS):
        vectors = panels[number]
        factor = factors[number]
        forward = jnp.dot(current, vectors, precision=lax.Precision.HIGHEST)
        scaled = jnp.dot(forward, factor, precision=lax.Precision.HIGHEST)
        projected = jnp.dot(vectors.T, scaled, precision=lax.Precision.HIGHEST)
        correct = jnp.dot(factor.T, projected, precision=lax.Precision.HIGHEST)
        weights = scaled - 0.5 * jnp.dot(vectors, correct, precision=lax.Precision.HIGHEST)
        current = current - jnp.dot(vectors, weights.T, precision=lax.Precision.HIGHEST)
        current = current - jnp.dot(weights, vectors.T, precision=lax.Precision.HIGHEST)
    return current
```

```python
import functools

import jax
import jax.numpy as jnp
from jax import lax
from jax.experimental import pallas as pl
from jax.experimental.pallas import tpu as pltpu
from jax.sharding import PartitionSpec as P

MESH = pl.DeviceIdType.MESH
F32 = jnp.float32
BF16 = jnp.bfloat16
NN = (((1,), (0,)), ((), ()))
NT = (((1,), (1,)), ((), ()))
TN = (((0,), (0,)), ((), ()))


def exact(a, b, dims=NN):
    return lax.dot_general(
        a, b, dims, precision=lax.Precision.HIGHEST, preferred_element_type=F32
    )


def halves(value):
    high = value.astype(BF16)
    return high, (value - high.astype(F32)).astype(BF16)


def dot3(a, b, dims=NN):
    (ah, al), (bh, bl) = a, b

    def one(p, q):
        return lax.dot_general(p, q, dims, preferred_element_type=F32)

    return one(ah, bh) + (one(ah, bl) + one(al, bh))


def exchange(nz, a_hbm, v_ref, f_ref, yc, vc, lh, ll,
             a_buf, v1, p_buf, rs, y1, yr, sp, srs, sf,
             a_sem, own_sem, g_send, g1_recv, g2_recv, g3_recv,
             rs_send, rs_recv, ag_send, ag_recv, ss_send, ss_recv, sg_send, sg_recv):
    row, col = lax.axis_index("row"), lax.axis_index("col")
    z, quad = row // 4, row % 4
    yl, core = quad // 2, quad % 2
    rows, width = a_buf.shape
    piece = rows // nz
    plane = 4 * nz
    srows = sp.shape[0] // plane
    mine = col * 4 + quad

    def at(ref, index, size):
        return ref.at[:, pl.ds(pl.multiple_of(index * size, 8), size), :]

    def send(src, dst, ssem, rsem, to_row, to_col):
        pltpu.make_async_remote_copy(
            src_ref=src, dst_ref=dst, send_sem=ssem, recv_sem=rsem,
            device_id=(to_row, to_col), device_id_type=MESH,
        ).start()

    def drain(ref, sem):
        pltpu.make_async_copy(ref, ref, sem).wait()

    load = pltpu.make_async_copy(a_hbm, a_buf, a_sem)
    load.start()
    own = pltpu.make_async_copy(at(v_ref, col, piece), at(v1, z, piece), own_sem)
    own.start()

    def zpeer(step):
        return (z + step) % nz

    def ppeer(step):
        other = (mine + step) % plane
        return z * 4 + other % 4, other // 4

    barrier = pltpu.get_barrier_semaphore()

    def greet_z(step, carry):
        pl.semaphore_signal(barrier, inc=1, device_id=(zpeer(step) * 4 + quad, col), device_id_type=MESH)
        return carry

    def greet_plane(step, carry):
        pl.semaphore_signal(barrier, inc=1, device_id=ppeer(step), device_id_type=MESH)
        return carry

    lax.fori_loop(1, nz, greet_z, 0)
    lax.fori_loop(1, plane, greet_plane, 0)
    pl.semaphore_wait(barrier, nz - 1 + plane - 1)

    def zorder(index):
        return (z + ((index % 2) * 2 - 1) * ((index + 1) // 2) + nz) % nz

    def spread(src, dst, which):
        def body(index, carry):
            to = zorder(nz - 1 - index)
            send(src, at(dst, z, piece), g_send.at[which, 0], g1_recv.at[which, z], to * 4 + quad, col)
            return carry

        lax.fori_loop(0, nz - 1, body, 0)

    def deliver(held, full, which):
        def body(index, carry):
            target = zorder(index)
            src = at(held, target, piece)

            @pl.when(index > 0)
            def _():
                drain(src, g1_recv.at[which, target])

            dst = full.at[:, pl.ds(pl.multiple_of(quad * rows + col * piece, 8), piece), :]

            send(src, dst, g_send.at[which, 1], g2_recv.at[which, yl], z * 4 + (1 - yl) * 2 + core, target)

            @pl.when(target != col)
            def _():
                send(src, dst, g_send.at[which, 2], g2_recv.at[which, yl], row, target)

            @pl.when(target == col)
            def _():
                pltpu.make_async_copy(src, dst, g2_recv.at[which, yl]).start()

            return carry

        lax.fori_loop(0, nz, body, 0)

    def relay(full, which):
        for side in range(2):
            block = at(full, side * 2 + core, rows)
            drain(block, g2_recv.at[which, side])
            send(block, block, g_send.at[which, 3 + side], g3_recv.at[which, side], z * 4 + yl * 2 + (1 - core), col)

    def partner(full, which, side):
        drain(at(full, side * 2 + (1 - core), rows), g3_recv.at[which, side])

    def settle(held, full, which):
        drain(at(held, 0, (nz - 1) * piece), g_send.at[which, 0])
        drain(at(held, 0, nz * piece), g_send.at[which, 1])
        drain(at(held, 0, (nz - 1) * piece), g_send.at[which, 2])
        for side in range(2):
            drain(at(full, 0, rows), g_send.at[which, 3 + side])

    own.wait()
    spread(at(v1, z, piece), v1, 0)
    deliver(v1, vc, 0)
    relay(vc, 0)
    load.wait()

    for side in range(2):
        partner(vc, 0, side)
        span = slice(side * 2 * rows, (side + 1) * 2 * rows)
        left = halves(a_buf[:, span])
        for panel in range(2):
            part = dot3(left, halves(vc[panel, span, :]))
            if side == 0:
                p_buf[panel] = part
            else:
                p_buf[panel] = p_buf[panel] + part

    def scatter(step, carry):
        to = (col + step) % nz
        send(at(p_buf, to, piece), at(rs, col, piece), rs_send, rs_recv, row, to)
        return carry

    lax.fori_loop(1, nz, scatter, 0)
    mine_rows = pl.ds(pl.multiple_of(col * piece, 8), piece)
    rs[:, mine_rows, :] = p_buf[:, mine_rows, :]
    drain(at(rs, 0, (nz - 1) * piece), rs_recv)
    total = rs[:, 0:piece, :]
    for other in range(1, nz):
        total = total + rs[:, other * piece:(other + 1) * piece, :]
    z_rows = pl.ds(pl.multiple_of(z * piece, 8), piece)
    y1[:, z_rows, :] = total
    yr[:, mine_rows, :] = total

    spread(at(y1, z, piece), y1, 1)

    def gather(step, carry):
        to = (col + step) % nz
        send(at(yr, col, piece), at(yr, col, piece), ag_send, ag_recv, row, to)
        return carry

    lax.fori_loop(1, nz, gather, 0)
    deliver(y1, yc, 1)

    half = sp.shape[0] // 2
    sp[:half, :half] = exact(v1[0], y1[0], TN)
    sp[:half, half:] = exact(v1[0], y1[1], TN)
    sp[half:, :half] = exact(v1[0], v1[1], TN)
    sp[half:, half:] = exact(v1[1], y1[1], TN)

    def split_sum(step, carry):
        to_row, to_col = ppeer(step)
        other = (mine + step) % plane
        send(sp.at[pl.ds(pl.multiple_of(other * srows, 8), srows), :], srs.at[mine], ss_send, ss_recv, to_row, to_col)
        return carry

    lax.fori_loop(1, plane, split_sum, 0)
    s_rows = pl.ds(pl.multiple_of(mine * srows, 8), srows)
    srs[mine] = sp[s_rows, :]
    relay(yc, 1)
    drain(srs.at[0:plane - 1], ss_recv)
    sf[s_rows, :] = jnp.sum(srs[...], axis=0)

    def join_sum(step, carry):
        to_row, to_col = ppeer(step)
        part = sf.at[s_rows, :]
        send(part, part, sg_send, sg_recv, to_row, to_col)
        return carry

    lax.fori_loop(1, plane, join_sum, 0)
    drain(at(yr, 0, (nz - 1) * piece), ag_recv)
    drain(sf.at[0:(plane - 1) * srows, :], sg_recv)

    f1, f2 = f_ref[0], f_ref[1]
    s11, s12 = sf[:half, :half], sf[:half, half:]
    gram, s22 = sf[half:, :half], sf[half:, half:]
    k1 = exact(exact(f1, s11, TN), f1)
    fs = exact(f1, s12, TN)
    kg = exact(k1, gram)
    mixed = exact(kg - fs, f2)
    cross = fs - 0.5 * kg
    gt = exact(gram, cross, TN)
    k2 = exact(exact(f2, s22 - gt - gt.T, TN), f2)
    e = exact(exact(f1, gram), f2)

    va, vb = v_ref[0], v_ref[1]
    ya, yb = yr[0], yr[1]
    parts = (
        exact(va, f1, NT) - exact(vb, e, NT),
        exact(vb, f2, NT),
        exact(ya, f1) - exact(va, k1) + exact(vb, mixed, NT),
        exact(yb, f2) - exact(ya, e) + exact(va, mixed) - exact(vb, k2),
    )
    for index, part in enumerate(parts):
        high, low = halves(part)
        lh[:, index * half:(index + 1) * half] = high
        ll[:, index * half:(index + 1) * half] = low

    for side in range(2):
        partner(yc, 1, side)
    settle(v1, vc, 0)
    settle(y1, yc, 1)
    drain(at(rs, 0, (nz - 1) * piece), rs_send)
    drain(at(rs, 0, (nz - 1) * piece), ag_send)
    drain(srs.at[0:plane - 1], ss_send)
    drain(srs.at[0:plane - 1], sg_send)


def apply_update(a_ref, yc, vc, lh, ll, out):
    right = jnp.concatenate([yc[0], yc[1], vc[0], vc[1]], axis=1)
    out[...] = a_ref[...] - dot3((lh[...], ll[...]), halves(right), NT)


def shards(nz, matrix, panels, factors):
    rows, width = matrix.shape
    size = panels.shape[2]
    piece = rows // nz
    srows = 2 * size // (4 * nz)
    vmem = pl.BlockSpec(memory_space=pltpu.VMEM)
    wide = jax.ShapeDtypeStruct((2, width, size), F32)
    left = jax.ShapeDtypeStruct((rows, 4 * size), BF16)
    block = pltpu.VMEM((2, rows, size), F32)
    dma = pltpu.SemaphoreType.DMA
    yc, vc, lh, ll = pl.pallas_call(
        functools.partial(exchange, nz),
        out_shape=(wide, wide, left, left),
        in_specs=[pl.BlockSpec(memory_space=pl.ANY), vmem, vmem],
        out_specs=(vmem, vmem, vmem, vmem),
        scratch_shapes=[
            pltpu.VMEM((rows, width), F32),
            block, block, block, block, block,
            pltpu.VMEM((2 * size, 2 * size), F32),
            pltpu.VMEM((4 * nz, srows, 2 * size), F32),
            pltpu.VMEM((2 * size, 2 * size), F32),
            dma(()), dma(()), dma((2, 5)), dma((2, nz)), dma((2, 2)), dma((2, 2)),
            dma(()), dma(()), dma(()), dma(()), dma(()), dma(()), dma(()), dma(()),
        ],
        compiler_params=pltpu.CompilerParams(collective_id=0, has_side_effects=True, vmem_limit_bytes=40 << 20),
        name="exchange",
    )(matrix, panels, factors)
    tile = 256 if width % 256 == 0 else width
    return pl.pallas_call(
        apply_update,
        grid=(width // tile,),
        out_shape=jax.ShapeDtypeStruct(matrix.shape, F32),
        in_specs=[
            pl.BlockSpec((rows, tile), lambda i: (0, i)),
            pl.BlockSpec((2, tile, size), lambda i: (0, i, 0)),
            pl.BlockSpec((2, tile, size), lambda i: (0, i, 0)),
            pl.BlockSpec((rows, 4 * size), lambda i: (0, 0)),
            pl.BlockSpec((rows, 4 * size), lambda i: (0, 0)),
        ],
        out_specs=pl.BlockSpec((rows, tile), lambda i: (0, i)),
        name="apply_update",
    )(matrix, yc, vc, lh, ll)


def solution(mesh):
    placed = (P("row", "col"), P(None, "row", None), P())
    return jax.shard_map(
        functools.partial(shards, mesh.shape["col"]),
        mesh=mesh, in_specs=placed, out_specs=P("row", "col"), check_vma=False,
    )
```

```python
import functools

import jax
import jax.numpy as jnp
from jax import lax
from jax.experimental import pallas as pl
from jax.experimental.pallas import tpu as pltpu
from jax.sharding import PartitionSpec as P

MESH = pl.DeviceIdType.MESH
F32 = jnp.float32
BF16 = jnp.bfloat16
NN = (((1,), (0,)), ((), ()))
NT = (((1,), (1,)), ((), ()))
TN = (((0,), (0,)), ((), ()))


def exact(a, b, dims=NN):
    return lax.dot_general(
        a, b, dims, precision=lax.Precision.HIGHEST, preferred_element_type=F32
    )


def halves(value):
    high = value.astype(BF16)
    return high, (value - high.astype(F32)).astype(BF16)


def dot3(a, b, dims=NN):
    (ah, al), (bh, bl) = a, b

    def one(p, q):
        return lax.dot_general(p, q, dims, preferred_element_type=F32)

    return one(ah, bh) + (one(ah, bl) + one(al, bh))


def exchange(nz, a_hbm, v_hbm, f_hbm, a_buf, rh, rl, lh, ll,
             ah, al, v_ref, f_ref, vc, yc, v1, p_buf, rs, y1, yr, sp, srs, szs, sf,
             a_sem, v_sem, f_sem, own_sem, g_send, g1_recv, g2_recv, g3_recv,
             rs_send, rs_recv, ag_send, ag_recv, ss_send, ss_recv, sg_send, sg_recv, sz_send, sz_recv):
    row, col = lax.axis_index("row"), lax.axis_index("col")
    z, quad = row // 4, row % 4
    yl, core = quad // 2, quad % 2
    rows, width = a_buf.shape
    piece = rows // nz
    plane = 4 * nz
    srows = sp.shape[0] // plane
    mine = col * 4 + quad

    def at(ref, index, size):
        return ref.at[:, pl.ds(pl.multiple_of(index * size, 8), size), :]

    def send(src, dst, ssem, rsem, to_row, to_col):
        pltpu.make_async_remote_copy(
            src_ref=src, dst_ref=dst, send_sem=ssem, recv_sem=rsem,
            device_id=(to_row, to_col), device_id_type=MESH,
        ).start()

    def drain(ref, sem):
        pltpu.make_async_copy(ref, ref, sem).wait()

    load_v = pltpu.make_async_copy(v_hbm, v_ref, v_sem)
    load_v.start()
    load_f = pltpu.make_async_copy(f_hbm, f_ref, f_sem)
    load_f.start()
    load = pltpu.make_async_copy(a_hbm, a_buf, a_sem)
    load.start()
    own = pltpu.make_async_copy(at(v_ref, col, piece), at(v1, z, piece), own_sem)
    def zpeer(step):
        return (z + step) % nz

    def ppeer(step):
        other = (mine + step) % plane
        return z * 4 + other % 4, other // 4

    barrier = pltpu.get_barrier_semaphore()

    def greet_z(step, carry):
        pl.semaphore_signal(barrier, inc=1, device_id=(zpeer(step) * 4 + quad, col), device_id_type=MESH)
        return carry

    def greet_plane(step, carry):
        pl.semaphore_signal(barrier, inc=1, device_id=ppeer(step), device_id_type=MESH)
        return carry

    lax.fori_loop(1, nz, greet_z, 0)
    lax.fori_loop(1, plane, greet_plane, 0)
    load_v.wait()
    own.start()
    own.wait()
    pl.semaphore_wait(barrier, nz - 1 + plane - 1)

    turn = col + 2 * quad

    def hop(index):
        return 1 + (index + turn) % (nz - 1)

    def spread(src, dst, which):
        def body(index, carry):
            to = (z + hop(index)) % nz
            send(src, at(dst, z, piece), g_send.at[which, 0], g1_recv.at[which, z], to * 4 + quad, col)
            return carry

        lax.fori_loop(0, nz - 1, body, 0)

    def hand_on(held, full, which, target):
        src = at(held, target, piece)
        dst = full.at[:, pl.ds(pl.multiple_of(quad * rows + col * piece, 8), piece), :]

        send(src, dst, g_send.at[which, 1], g2_recv.at[which, yl], z * 4 + (1 - yl) * 2 + core, target)

        @pl.when(target != col)
        def _():
            send(src, dst, g_send.at[which, 2], g2_recv.at[which, yl], row, target)

        @pl.when(target == col)
        def _():
            pltpu.make_async_copy(src, dst, g2_recv.at[which, yl]).start()

    def deliver(held, full, which, first, last):
        def body(index, carry):
            target = (z + nz - hop(index)) % nz
            drain(at(held, target, piece), g1_recv.at[which, target])
            hand_on(held, full, which, target)
            return carry

        lax.fori_loop(first, last, body, 0)

    def relay(full, which):
        for side in range(2):
            block = at(full, side * 2 + core, rows)
            drain(block, g2_recv.at[which, side])
            send(block, block, g_send.at[which, 3 + side], g3_recv.at[which, side], z * 4 + yl * 2 + (1 - core), col)

    def partner(full, which, side):
        drain(at(full, side * 2 + (1 - core), rows), g3_recv.at[which, side])

    def settle(held, full, which):
        drain(at(held, 0, (nz - 1) * piece), g_send.at[which, 0])
        drain(at(held, 0, nz * piece), g_send.at[which, 1])
        drain(at(held, 0, (nz - 1) * piece), g_send.at[which, 2])
        for side in range(2):
            drain(at(full, 0, rows), g_send.at[which, 3 + side])

    half = v_ref.shape[2]

    def split_into(full, base):
        for panel in range(2):
            high, low = halves(full[panel])
            rh[:, base + panel * half:base + (panel + 1) * half] = high
            rl[:, base + panel * half:base + (panel + 1) * half] = low

    spread(at(v1, z, piece), v1, 0)
    hand_on(v1, vc, 0, z)
    load.wait()
    ah[...], al[...] = halves(a_buf[...])
    deliver(v1, vc, 0, 0, nz - 1)
    relay(vc, 0)

    for side in range(2):
        partner(vc, 0, side)
        span = slice(side * 2 * rows, (side + 1) * 2 * rows)
        for panel in range(2):
            high, low = halves(vc[panel, span, :])
            rh[span, (2 + panel) * half:(3 + panel) * half] = high
            rl[span, (2 + panel) * half:(3 + panel) * half] = low
        part = dot3((ah[:, span], al[:, span]), (rh[span, 2 * half:], rl[span, 2 * half:]))
        for panel in range(2):
            one = part[:, panel * half:(panel + 1) * half]
            p_buf[panel] = one if side == 0 else p_buf[panel] + one

    def scatter(step, carry):
        to = (col + step) % nz
        send(at(p_buf, to, piece), at(rs, col, piece), rs_send, rs_recv, row, to)
        return carry

    lax.fori_loop(1, nz, scatter, 0)
    mine_rows = pl.ds(pl.multiple_of(col * piece, 8), piece)
    rs[:, mine_rows, :] = p_buf[:, mine_rows, :]
    drain(at(rs, 0, (nz - 1) * piece), rs_recv)
    total = rs[:, 0:piece, :]
    for other in range(1, nz):
        total = total + rs[:, other * piece:(other + 1) * piece, :]
    z_rows = pl.ds(pl.multiple_of(z * piece, 8), piece)
    y1[:, z_rows, :] = total
    yr[:, mine_rows, :] = total

    spread(at(y1, z, piece), y1, 1)

    hand_on(y1, yc, 1, z)

    va, vb = v_ref[0, mine_rows, :], v_ref[1, mine_rows, :]
    sp[:half, :half] = exact(va, total[0], TN)
    sp[:half, half:] = exact(va, total[1], TN)
    sp[half:, :half] = exact(va, vb, TN)
    sp[half:, half:] = exact(vb, total[1], TN)

    def split_sum(step, carry):
        to_row, to_col = ppeer(step)
        other = (mine + step) % plane
        send(sp.at[pl.ds(pl.multiple_of(other * srows, 8), srows), :], srs.at[mine], ss_send, ss_recv, to_row, to_col)
        return carry

    lax.fori_loop(1, plane, split_sum, 0)
    s_rows = pl.ds(pl.multiple_of(mine * srows, 8), srows)
    srs[mine] = sp[s_rows, :]

    def gather(step, carry):
        to = (col + step) % nz
        send(at(yr, col, piece), at(yr, col, piece), ag_send, ag_recv, row, to)
        return carry

    lax.fori_loop(1, nz, gather, 0)
    cuts = (nz - 1) // 3, 2 * (nz - 1) // 3
    deliver(y1, yc, 1, 0, cuts[0])
    drain(srs.at[0:plane - 1], ss_recv)
    szs[z] = jnp.sum(srs[...], axis=0)

    def level(step, carry):
        send(szs.at[z], szs.at[z], sz_send, sz_recv, zpeer(step) * 4 + quad, col)
        return carry

    lax.fori_loop(1, nz, level, 0)
    deliver(y1, yc, 1, cuts[0], cuts[1])
    drain(szs.at[0:nz - 1], sz_recv)
    sf[s_rows, :] = jnp.sum(szs[...], axis=0)

    def join_sum(step, carry):
        to_row, to_col = ppeer(step)
        part = sf.at[s_rows, :]
        send(part, part, sg_send, sg_recv, to_row, to_col)
        return carry

    lax.fori_loop(1, plane, join_sum, 0)
    deliver(y1, yc, 1, cuts[1], nz - 1)
    relay(yc, 1)
    drain(at(yr, 0, (nz - 1) * piece), ag_recv)
    drain(sf.at[0:(plane - 1) * srows, :], sg_recv)

    load_f.wait()
    f1, f2 = f_ref[0], f_ref[1]
    s11, s12 = sf[:half, :half], sf[:half, half:]
    gram, s22 = sf[half:, :half], sf[half:, half:]
    k1 = exact(exact(f1, s11, TN), f1)
    fs = exact(f1, s12, TN)
    kg = exact(k1, gram)
    mixed = exact(kg - fs, f2)
    cross = fs - 0.5 * kg
    gt = exact(gram, cross, TN)
    k2 = exact(exact(f2, s22 - gt - gt.T, TN), f2)
    e = exact(exact(f1, gram), f2)

    va, vb = v_ref[0], v_ref[1]
    ya, yb = yr[0], yr[1]
    parts = (
        exact(va, f1, NT) - exact(vb, e, NT),
        exact(vb, f2, NT),
        exact(ya, f1) - exact(va, k1) + exact(vb, mixed, NT),
        exact(yb, f2) - exact(ya, e) + exact(va, mixed) - exact(vb, k2),
    )
    for index, part in enumerate(parts):
        high, low = halves(part)
        lh[:, index * half:(index + 1) * half] = high
        ll[:, index * half:(index + 1) * half] = low

    for side in range(2):
        partner(yc, 1, side)
    split_into(yc, 0)
    settle(v1, vc, 0)
    settle(y1, yc, 1)
    drain(at(rs, 0, (nz - 1) * piece), rs_send)
    drain(at(rs, 0, (nz - 1) * piece), ag_send)
    drain(srs.at[0:plane - 1], ss_send)
    drain(srs.at[0:plane - 1], sg_send)
    drain(szs.at[0:nz - 1], sz_send)


def apply_update(tile, a_ref, rh, rl, lh, ll, out, stage, sems):
    count = out.shape[1] // tile

    def store(slot, index):
        span = pl.ds(pl.multiple_of(index * tile, tile), tile)
        return pltpu.make_async_copy(stage.at[slot], out.at[:, span], sems.at[slot])

    def body(index, carry):
        slot = index % 2

        @pl.when(index >= 2)
        def _():
            store(slot, index - 2).wait()

        span = pl.ds(pl.multiple_of(index * tile, tile), tile)
        stage[slot] = a_ref[:, span] - dot3((lh[...], ll[...]), (rh[span, :], rl[span, :]), NT)
        store(slot, index).start()
        return carry

    lax.fori_loop(0, count, body, 0)
    for index in range(max(count - 2, 0), count):
        store(index % 2, index).wait()


def shards(nz, matrix, panels, factors):
    rows, width = matrix.shape
    size = panels.shape[2]
    srows = 2 * size // (4 * nz)
    vmem = pl.BlockSpec(memory_space=pltpu.VMEM)
    hbm = pl.BlockSpec(memory_space=pltpu.HBM)
    right = jax.ShapeDtypeStruct((width, 4 * size), BF16)
    left = jax.ShapeDtypeStruct((rows, 4 * size), BF16)
    block = pltpu.VMEM((2, rows, size), F32)
    wide = pltpu.VMEM((2, width, size), F32)
    square = pltpu.VMEM((2 * size, 2 * size), F32)
    dma = pltpu.SemaphoreType.DMA
    held = pl.pallas_call(
        functools.partial(exchange, nz),
        out_shape=(jax.ShapeDtypeStruct(matrix.shape, F32), right, right, left, left),
        in_specs=[hbm, hbm, hbm],
        out_specs=(vmem,) * 5,
        scratch_shapes=[
            pltpu.VMEM((rows, width), BF16), pltpu.VMEM((rows, width), BF16),
            block, pltpu.VMEM(factors.shape, F32), wide, wide,
            block, block, block, block, block,
            square, pltpu.VMEM((4 * nz, srows, 2 * size), F32),
            pltpu.VMEM((nz, srows, 2 * size), F32), square,
            dma(()), dma(()), dma(()), dma(()), dma((2, 5)), dma((2, nz)), dma((2, 2)), dma((2, 2)),
        ] + [dma(())] * 10,
        compiler_params=pltpu.CompilerParams(collective_id=0, has_side_effects=True, vmem_limit_bytes=40 << 20),
        name="exchange",
    )(matrix, panels, factors)
    tile = 256 if width % 256 == 0 else width
    return pl.pallas_call(
        functools.partial(apply_update, tile),
        out_shape=jax.ShapeDtypeStruct(matrix.shape, F32),
        in_specs=[vmem] * 5,
        out_specs=hbm,
        scratch_shapes=[pltpu.VMEM((2, rows, tile), F32), dma((2,))],
        compiler_params=pltpu.CompilerParams(vmem_limit_bytes=24 << 20),
        name="apply_update",
    )(*held)


def solution(mesh):
    placed = (P("row", "col"), P(None, "row", None), P())
    return jax.shard_map(
        functools.partial(shards, mesh.shape["col"]),
        mesh=mesh, in_specs=placed, out_specs=P("row", "col"), check_vma=False,
    )
```

```python
import functools

import jax
import jax.numpy as jnp
from jax import lax
from jax.experimental import pallas as pl
from jax.experimental.pallas import tpu as pltpu
from jax.sharding import PartitionSpec as P

MESH = pl.DeviceIdType.MESH
F32 = jnp.float32
BF16 = jnp.bfloat16
NN = (((1,), (0,)), ((), ()))
NT = (((1,), (1,)), ((), ()))
TN = (((0,), (0,)), ((), ()))


def exact(a, b, dims=NN):
    return lax.dot_general(
        a, b, dims, precision=lax.Precision.HIGHEST, preferred_element_type=F32
    )


def halves(value):
    high = value.astype(BF16)
    return high, (value - high.astype(F32)).astype(BF16)


def exchange(nz, a_hbm, v_hbm, f_hbm, a_buf, right, lh, ll,
             ah, al, v_ref, f_ref, vc, yc, v1, p_buf, rs, y1, yr, sp, srs, szs, sf,
             a_sem, v_sem, f_sem, own_sem, g_send, g1_recv, g2_recv, g3_recv,
             rs_send, rs_recv, ag_send, ag_recv, ss_send, ss_recv, sg_send, sg_recv, sz_send, sz_recv):
    row, col = lax.axis_index("row"), lax.axis_index("col")
    z, quad = row // 4, row % 4
    yl, core = quad // 2, quad % 2
    rows, width = a_buf.shape
    size = v_ref.shape[2]
    piece = rows // nz
    plane = 4 * nz
    srows = sp.shape[1] // plane
    mine = col * 4 + quad

    def block(index, step):
        return pl.ds(pl.multiple_of(index * step, 8), step)

    def send(src, dst, ssem, rsem, to_row, to_col):
        pltpu.make_async_remote_copy(
            src_ref=src, dst_ref=dst, send_sem=ssem, recv_sem=rsem,
            device_id=(to_row, to_col), device_id_type=MESH,
        ).start()

    def drain(ref, sem):
        pltpu.make_async_copy(ref, ref, sem).wait()

    load_v = pltpu.make_async_copy(v_hbm, v_ref, v_sem)
    load_v.start()
    load_f = pltpu.make_async_copy(f_hbm, f_ref, f_sem)
    load_f.start()
    load = pltpu.make_async_copy(a_hbm, a_buf, a_sem)
    load.start()
    mine_rows, z_rows, s_rows = block(col, piece), block(z, piece), block(mine, srows)
    own = pltpu.make_async_copy(v_ref.at[:, mine_rows, :], v1.at[:, z_rows, :], own_sem)

    def zpeer(step):
        return (z + step) % nz

    def ppeer(step):
        other = (mine + step) % plane
        return z * 4 + other % 4, other // 4

    barrier = pltpu.get_barrier_semaphore()

    def greet_z(step, carry):
        pl.semaphore_signal(barrier, inc=1, device_id=(zpeer(step) * 4 + quad, col), device_id_type=MESH)
        return carry

    def greet_plane(step, carry):
        pl.semaphore_signal(barrier, inc=1, device_id=ppeer(step), device_id_type=MESH)
        return carry

    lax.fori_loop(1, nz, greet_z, 0)
    lax.fori_loop(1, plane, greet_plane, 0)
    load_v.wait()
    own.start()
    own.wait()
    pl.semaphore_wait(barrier, nz - 1 + plane - 1)

    turn = col + 2 * quad

    def hop(index):
        return (index + turn) % nz

    def spread(held, which):
        part = held.at[z_rows, :]

        def body(index, carry):
            to = (z + hop(index)) % nz

            @pl.when(to != z)
            def _():
                send(part, part, g_send.at[which, 0], g1_recv.at[which, z], to * 4 + quad, col)

            return carry

        lax.fori_loop(0, nz, body, 0)

    def hand_on(held, full, which, target):
        src = held.at[block(target, piece), :]
        dst = full.at[pl.ds(pl.multiple_of(quad * rows + col * piece, 8), piece), :]
        send(src, dst, g_send.at[which, 1], g2_recv.at[which, yl], z * 4 + (1 - yl) * 2 + core, target)

        @pl.when(target != col)
        def _():
            send(src, dst, g_send.at[which, 2], g2_recv.at[which, yl], row, target)

        @pl.when(target == col)
        def _():
            pltpu.make_async_copy(src, dst, g2_recv.at[which, yl]).start()

    def deliver(held, full, which, first, last):
        def body(index, carry):
            target = (z + nz - hop(index)) % nz

            @pl.when(target != z)
            def _():
                drain(held.at[block(target, piece), :], g1_recv.at[which, target])

            hand_on(held, full, which, target)
            return carry

        lax.fori_loop(first, last, body, 0)

    def relay(full, which):
        for side in range(2):
            part = full.at[block(side * 2 + core, rows), :]
            drain(part, g2_recv.at[which, side])
            send(part, part, g_send.at[which, 3 + side], g3_recv.at[which, side], z * 4 + yl * 2 + (1 - core), col)

    def partner(full, which, side):
        drain(full.at[block(side * 2 + (1 - core), rows), :], g3_recv.at[which, side])

    def settle(held, full, which):
        drain(held.at[0:(nz - 1) * piece, :], g_send.at[which, 0])
        drain(held.at[0:nz * piece, :], g_send.at[which, 1])
        drain(held.at[0:(nz - 1) * piece, :], g_send.at[which, 2])
        for side in range(2):
            drain(full.at[0:rows, :], g_send.at[which, 3 + side])

    def sum_start(group):
        def body(step, carry):
            to_row, to_col = ppeer(step)
            other = (mine + step) % plane
            send(sp.at[group, block(other, srows), :], srs.at[group, mine], ss_send.at[group], ss_recv.at[group], to_row, to_col)
            return carry

        lax.fori_loop(1, plane, body, 0)
        srs[group, mine] = sp[group, s_rows, :]

    def sum_level(group):
        drain(srs.at[group, 0:plane - 1], ss_recv.at[group])
        szs[group, z] = jnp.sum(srs[group], axis=0)

        def body(step, carry):
            part = szs.at[group, z]
            send(part, part, sz_send.at[group], sz_recv.at[group], zpeer(step) * 4 + quad, col)
            return carry

        lax.fori_loop(1, nz, body, 0)

    def sum_share(group):
        drain(szs.at[group, 0:nz - 1], sz_recv.at[group])
        sf[group, s_rows, :] = jnp.sum(szs[group], axis=0)

        def body(step, carry):
            to_row, to_col = ppeer(step)
            part = sf.at[group, s_rows, :]
            send(part, part, sg_send.at[group], sg_recv.at[group], to_row, to_col)
            return carry

        lax.fori_loop(1, plane, body, 0)

    def sum_end(group):
        drain(sf.at[group, 0:(plane - 1) * srows, :], sg_recv.at[group])

    def sum_settle(group):
        drain(srs.at[group, 0:plane - 1], ss_send.at[group])
        drain(szs.at[group, 0:nz - 1], sz_send.at[group])
        drain(srs.at[group, 0:plane - 1], sg_send.at[group])

    for panel in range(2):
        spread(v1.at[panel], panel)
    va, vb = v_ref[0, mine_rows, :], v_ref[1, mine_rows, :]
    sp[0, :size] = exact(va, vb, TN)
    sp[0, size:] = sp[0, :size]
    sum_start(0)
    load.wait()
    ah[...], al[...] = halves(a_buf[...])
    deliver(v1.at[0], vc.at[0], 0, 0, nz)
    deliver(v1.at[1], vc.at[1], 1, 0, nz)
    sum_level(0)

    def fold(full, slot, span):
        high, low = halves(full[span, :])
        right[span, 2 * slot * size:(2 * slot + 1) * size] = high
        right[span, (2 * slot + 1) * size:(2 * slot + 2) * size] = low

    for panel in range(2):
        relay(vc.at[panel], panel)
        slot = 2 + panel
        base = 2 * slot * size
        for side in range(2):
            partner(vc.at[panel], panel, side)
            span = slice(side * 2 * rows, (side + 1) * 2 * rows)
            fold(vc.at[panel], slot, span)
            both = lax.dot_general(ah[:, span], right[span, base:base + 2 * size], NN, preferred_element_type=F32)
            part = lax.dot_general(al[:, span], right[span, base:base + size], NN, preferred_element_type=F32)
            part = part + both[:, size:] + both[:, :size]
            p_buf[panel] = part if side == 0 else p_buf[panel] + part

        def scatter(step, carry, panel=panel):
            to = (col + step) % nz
            send(p_buf.at[panel, block(to, piece), :], rs.at[panel, mine_rows, :], rs_send.at[panel], rs_recv.at[panel], row, to)
            return carry

        lax.fori_loop(1, nz, scatter, 0)
        rs[panel, mine_rows, :] = p_buf[panel, mine_rows, :]
    sum_share(0)

    for panel in range(2):
        drain(rs.at[panel, 0:(nz - 1) * piece, :], rs_recv.at[panel])
        total = rs[panel, 0:piece, :]
        for other in range(1, nz):
            total = total + rs[panel, other * piece:(other + 1) * piece, :]
        y1[panel, z_rows, :] = total
        yr[panel, mine_rows, :] = total
        spread(y1.at[panel], 2 + panel)
        sp[1 + panel, :size] = exact(vb if panel else va, total, TN)
        sp[1 + panel, size:] = exact(vb, total, TN)
        sum_start(1 + panel)

    def gather_all(panel):
        def body(step, carry):
            to = (col + step) % nz
            part = yr.at[panel, mine_rows, :]
            send(part, part, ag_send.at[panel], ag_recv.at[panel], row, to)
            return carry

        lax.fori_loop(1, nz, body, 0)

    deliver(y1.at[0], yc.at[0], 2, 0, nz)
    sum_level(1)
    gather_all(0)
    deliver(y1.at[1], yc.at[1], 3, 0, nz)
    sum_level(2)
    gather_all(1)
    sum_share(1)
    relay(yc.at[0], 2)
    sum_share(2)

    load_f.wait()
    f1, f2 = f_ref[0], f_ref[1]
    va, vb = v_ref[0], v_ref[1]
    sum_end(0)
    gram = sf[0, :size]
    gf = exact(gram, f2)
    e = exact(f1, gf)
    lefts = [exact(va, f1, NT) - exact(vb, e, NT), exact(vb, f2, NT)]
    for panel in range(2):
        drain(yr.at[panel, 0:(nz - 1) * piece, :], ag_recv.at[panel])
    ya, yb = yr[0], yr[1]
    sum_end(1)
    s11, s21 = sf[1, :size], sf[1, size:]
    k1 = exact(exact(f1, s11, TN), f1)
    fs = exact(f1, s21, (((0,), (1,)), ((), ())))
    kg = exact(k1, gram)
    mixed = exact(kg - fs, f2)
    gt = exact(gram, fs - 0.5 * kg, TN)
    lefts.append(exact(ya, f1) - exact(va, k1) + exact(vb, mixed, NT))
    rest = exact(yb, f2) - exact(ya, e) + exact(va, mixed)
    for panel in range(2):
        if panel:
            relay(yc.at[1], 3)
        for side in range(2):
            partner(yc.at[panel], 2 + panel, side)
        fold(yc.at[panel], panel, slice(0, width))
    sum_end(2)
    k2 = exact(exact(f2, sf[2, :size] - gt - gt.T, TN), f2)
    lefts.append(rest - exact(vb, k2))
    for index, part in enumerate(lefts):
        high, low = halves(part)
        lh[:, 2 * index * size:(2 * index + 1) * size] = high
        lh[:, (2 * index + 1) * size:(2 * index + 2) * size] = high
        ll[:, index * size:(index + 1) * size] = low

    for panel in range(2):
        settle(v1.at[panel], vc.at[panel], panel)
        settle(y1.at[panel], yc.at[panel], 2 + panel)
        drain(rs.at[panel, 0:(nz - 1) * piece, :], rs_send.at[panel])
        drain(rs.at[panel, 0:(nz - 1) * piece, :], ag_send.at[panel])
    for group in range(3):
        sum_settle(group)


def apply_update(tile, size, a_ref, right, lh, ll, out, stage, sems):
    count = out.shape[1] // tile

    def store(slot, index):
        span = pl.ds(pl.multiple_of(index * tile, tile), tile)
        return pltpu.make_async_copy(stage.at[slot], out.at[:, span], sems.at[slot])

    def body(index, carry):
        slot = index % 2

        @pl.when(index >= 2)
        def _():
            store(slot, index - 2).wait()

        span = pl.ds(pl.multiple_of(index * tile, tile), tile)
        highs = jnp.concatenate([right[span, 2 * s * size:(2 * s + 1) * size] for s in range(4)], axis=1)
        drop = lax.dot_general(ll[...], highs, NT, preferred_element_type=F32)
        drop = drop + lax.dot_general(lh[...], right[span, :], NT, preferred_element_type=F32)
        stage[slot] = a_ref[:, span] - drop
        store(slot, index).start()
        return carry

    lax.fori_loop(0, count, body, 0)
    for index in range(max(count - 2, 0), count):
        store(index % 2, index).wait()


def shards(nz, matrix, panels, factors):
    rows, width = matrix.shape
    size = panels.shape[2]
    srows = 2 * size // (4 * nz)
    vmem = pl.BlockSpec(memory_space=pltpu.VMEM)
    hbm = pl.BlockSpec(memory_space=pltpu.HBM)
    block = pltpu.VMEM((2, rows, size), F32)
    wide = pltpu.VMEM((2, width, size), F32)
    sums = pltpu.VMEM((3, 2 * size, size), F32)
    dma = pltpu.SemaphoreType.DMA
    held = pl.pallas_call(
        functools.partial(exchange, nz),
        out_shape=(
            jax.ShapeDtypeStruct(matrix.shape, F32),
            jax.ShapeDtypeStruct((width, 8 * size), BF16),
            jax.ShapeDtypeStruct((rows, 8 * size), BF16),
            jax.ShapeDtypeStruct((rows, 4 * size), BF16),
        ),
        in_specs=[hbm, hbm, hbm],
        out_specs=(vmem,) * 4,
        scratch_shapes=[
            pltpu.VMEM((rows, width), BF16), pltpu.VMEM((rows, width), BF16),
            block, pltpu.VMEM(factors.shape, F32), wide, wide,
            block, block, block, block, block,
            sums, pltpu.VMEM((3, 4 * nz, srows, size), F32),
            pltpu.VMEM((3, nz, srows, size), F32), sums,
            dma(()), dma(()), dma(()), dma(()), dma((4, 5)), dma((4, nz)), dma((4, 2)), dma((4, 2)),
        ] + [dma((2,))] * 4 + [dma((3,))] * 6,
        compiler_params=pltpu.CompilerParams(collective_id=0, has_side_effects=True, vmem_limit_bytes=40 << 20),
        name="exchange",
    )(matrix, panels, factors)
    tile = 256 if width % 256 == 0 else width
    return pl.pallas_call(
        functools.partial(apply_update, tile, size),
        out_shape=jax.ShapeDtypeStruct(matrix.shape, F32),
        in_specs=[vmem] * 4,
        out_specs=hbm,
        scratch_shapes=[pltpu.VMEM((2, rows, tile), F32), dma((2,))],
        compiler_params=pltpu.CompilerParams(vmem_limit_bytes=24 << 20),
        name="apply_update",
    )(*held)


def solution(mesh):
    placed = (P("row", "col"), P(None, "row", None), P())
    return jax.shard_map(
        functools.partial(shards, mesh.shape["col"]),
        mesh=mesh, in_specs=placed, out_specs=P("row", "col"), check_vma=False,
    )
```

```python
import functools

import jax
import jax.numpy as jnp
from jax import lax
from jax.experimental import pallas as pl
from jax.experimental.pallas import tpu as pltpu
from jax.sharding import PartitionSpec as P

MESH = pl.DeviceIdType.MESH
F32 = jnp.float32
BF16 = jnp.bfloat16
NN = (((1,), (0,)), ((), ()))
NT = (((1,), (1,)), ((), ()))
TN = (((0,), (0,)), ((), ()))


def exact(a, b, dims=NN):
    return lax.dot_general(
        a, b, dims, precision=lax.Precision.HIGHEST, preferred_element_type=F32
    )


def halves(value):
    high = value.astype(BF16)
    return high, (value - high.astype(F32)).astype(BF16)


def drop(left, low, right, span):
    size = right.shape[1] // 4
    highs = jnp.concatenate([right[span, 0:size], right[span, 2 * size:3 * size]], axis=1)
    value = lax.dot_general(low[...], highs, NT, preferred_element_type=F32)
    return value + lax.dot_general(left[...], right[span, :], NT, preferred_element_type=F32)


def exchange(nz, tile, a_hbm, v_hbm, f_hbm, a_buf, right_b, lh_b, ll_b,
             right_a, lh_a, ll_a, ah, al, v_ref, f_ref, vc, yc, v1, p_buf, rs, y1, yr, sp, srs, szs, sf,
             a_sem, v_sem, f_sem, own_sem, g_send, g1_recv, g2_recv, g3_recv,
             rs_send, rs_recv, ag_send, ag_recv, ap_recv, ss_send, ss_recv, sg_send, sg_recv, sz_send, sz_recv):
    row, col = lax.axis_index("row"), lax.axis_index("col")
    z, quad = row // 4, row % 4
    yl, core = quad // 2, quad % 2
    rows, width = a_buf.shape
    size = v_ref.shape[2]
    piece = rows // nz
    plane = 4 * nz
    srows = sp.shape[1] // plane
    mine = col * 4 + quad

    def block(index, step):
        return pl.ds(pl.multiple_of(index * step, 8), step)

    def send(src, dst, ssem, rsem, to_row, to_col):
        pltpu.make_async_remote_copy(
            src_ref=src, dst_ref=dst, send_sem=ssem, recv_sem=rsem,
            device_id=(to_row, to_col), device_id_type=MESH,
        ).start()

    def drain(ref, sem):
        pltpu.make_async_copy(ref, ref, sem).wait()

    load_v = pltpu.make_async_copy(v_hbm, v_ref, v_sem)
    load_v.start()
    load_f = pltpu.make_async_copy(f_hbm, f_ref, f_sem)
    load_f.start()
    load = pltpu.make_async_copy(a_hbm, a_buf, a_sem)
    load.start()
    mine_rows, z_rows, s_rows = block(col, piece), block(z, piece), block(mine, srows)
    own = pltpu.make_async_copy(v_ref.at[:, mine_rows, :], v1.at[:, z_rows, :], own_sem)

    def zpeer(step):
        return (z + step) % nz

    def ppeer(step):
        other = (mine + step) % plane
        return z * 4 + other % 4, other // 4

    barrier = pltpu.get_barrier_semaphore()

    def greet_z(step, carry):
        pl.semaphore_signal(barrier, inc=1, device_id=(zpeer(step) * 4 + quad, col), device_id_type=MESH)
        return carry

    def greet_plane(step, carry):
        pl.semaphore_signal(barrier, inc=1, device_id=ppeer(step), device_id_type=MESH)
        return carry

    lax.fori_loop(1, nz, greet_z, 0)
    lax.fori_loop(1, plane, greet_plane, 0)
    load_v.wait()
    own.start()
    own.wait()
    pl.semaphore_wait(barrier, nz - 1 + plane - 1)

    turn = col + 2 * quad

    def hop(index):
        return (index + turn) % nz

    def spread_one(held, which, index):
        part = held.at[z_rows, :]
        to = (z + hop(index)) % nz

        @pl.when(to != z)
        def _():
            send(part, part, g_send.at[which, 0], g1_recv.at[which, z], to * 4 + quad, col)

    def spread(held, which):
        def body(index, carry):
            spread_one(held, which, index)
            return carry

        lax.fori_loop(0, nz, body, 0)

    def hand_on(held, full, which, target):
        src = held.at[block(target, piece), :]
        dst = full.at[pl.ds(pl.multiple_of(quad * rows + col * piece, 8), piece), :]
        send(src, dst, g_send.at[which, 1], g2_recv.at[which, yl], z * 4 + (1 - yl) * 2 + core, target)

        @pl.when(target != col)
        def _():
            send(src, dst, g_send.at[which, 2], g2_recv.at[which, yl], row, target)

        @pl.when(target == col)
        def _():
            pltpu.make_async_copy(src, dst, g2_recv.at[which, yl]).start()

    def deliver(held, full, which, first, last, following=None):
        def body(index, carry):
            target = (z + nz - hop(index)) % nz

            @pl.when(target != z)
            def _():
                drain(held.at[block(target, piece), :], g1_recv.at[which, target])

            hand_on(held, full, which, target)
            if following is not None:
                spread_one(following, which + 1, index)
            return carry

        lax.fori_loop(first, last, body, 0)

    def relay(full, which):
        for side in range(2):
            part = full.at[block(side * 2 + core, rows), :]
            drain(part, g2_recv.at[which, side])
            send(part, part, g_send.at[which, 3 + side], g3_recv.at[which, side], z * 4 + yl * 2 + (1 - core), col)

    def partner(full, which, side):
        drain(full.at[block(side * 2 + (1 - core), rows), :], g3_recv.at[which, side])

    def settle(held, full, which):
        drain(held.at[0:(nz - 1) * piece, :], g_send.at[which, 0])
        drain(held.at[0:nz * piece, :], g_send.at[which, 1])
        drain(held.at[0:(nz - 1) * piece, :], g_send.at[which, 2])
        for side in range(2):
            drain(full.at[0:rows, :], g_send.at[which, 3 + side])

    def sum_start(group):
        def body(step, carry):
            to_row, to_col = ppeer(step)
            other = (mine + step) % plane
            send(sp.at[group, block(other, srows), :], srs.at[group, mine], ss_send.at[group], ss_recv.at[group], to_row, to_col)
            return carry

        lax.fori_loop(1, plane, body, 0)
        srs[group, mine] = sp[group, s_rows, :]

    def sum_level(group):
        drain(srs.at[group, 0:plane - 1], ss_recv.at[group])
        szs[group, z] = jnp.sum(srs[group], axis=0)

        def body(step, carry):
            part = szs.at[group, z]
            send(part, part, sz_send.at[group], sz_recv.at[group], zpeer(step) * 4 + quad, col)
            return carry

        lax.fori_loop(1, nz, body, 0)

    def sum_share(group):
        drain(szs.at[group, 0:nz - 1], sz_recv.at[group])
        sf[group, s_rows, :] = jnp.sum(szs[group], axis=0)

        def body(step, carry):
            to_row, to_col = ppeer(step)
            part = sf.at[group, s_rows, :]
            send(part, part, sg_send.at[group], sg_recv.at[group], to_row, to_col)
            return carry

        lax.fori_loop(1, plane, body, 0)

    def sum_end(group):
        drain(sf.at[group, 0:(plane - 1) * srows, :], sg_recv.at[group])

    def sum_settle(group):
        drain(srs.at[group, 0:plane - 1], ss_send.at[group])
        drain(szs.at[group, 0:nz - 1], sz_send.at[group])
        drain(srs.at[group, 0:plane - 1], sg_send.at[group])

    spread(v1.at[0], 0)
    na, nb = v_ref[0, mine_rows, :], v_ref[1, mine_rows, :]
    sp[0, :size] = exact(na, nb, TN)
    sp[0, size:] = sp[0, :size]
    sum_start(0)
    load.wait()
    ah[...], al[...] = halves(a_buf[...])
    deliver(v1.at[0], vc.at[0], 0, 0, nz, v1.at[1])
    deliver(v1.at[1], vc.at[1], 1, 0, nz // 2)
    relay(vc.at[0], 0)
    deliver(v1.at[1], vc.at[1], 1, nz // 2, nz)
    sum_level(0)

    rights = (right_a, right_b)

    def fold(full, panel, base, span):
        high, low = halves(full[span, :])
        rights[panel][span, base:base + size] = high
        rights[panel][span, base + size:base + 2 * size] = low

    for panel in range(2):
        if panel:
            relay(vc.at[1], 1)
            sum_share(0)
        held = rights[panel]
        for side in range(2):
            partner(vc.at[panel], panel, side)
            span = slice(side * 2 * rows, (side + 1) * 2 * rows)
            fold(vc.at[panel], panel, 2 * size, span)
            both = lax.dot_general(ah[:, span], held[span, 2 * size:], NN, preferred_element_type=F32)
            part = lax.dot_general(al[:, span], held[span, 2 * size:3 * size], NN, preferred_element_type=F32)
            part = part + both[:, size:] + both[:, :size]
            p_buf[panel] = part if side == 0 else p_buf[panel] + part

        def scatter(step, carry, panel=panel):
            to = (col + step) % nz
            send(p_buf.at[panel, block(to, piece), :], rs.at[panel, mine_rows, :], rs_send.at[panel], rs_recv.at[panel], row, to)
            return carry

        lax.fori_loop(1, nz, scatter, 0)
        rs[panel, mine_rows, :] = p_buf[panel, mine_rows, :]

    xn = nz // 2
    facing = (col + xn) % nz

    def gather_send(panel, owner, with_facing):
        part = yr.at[panel, block(owner, piece), :]
        if with_facing:
            send(part, part, ag_send.at[panel], ap_recv.at[panel], row, facing)

        def body(step, carry):
            to = (col // xn) * xn + (col + step) % xn
            send(part, part, ag_send.at[panel], ag_recv.at[panel], row, to)
            return carry

        lax.fori_loop(1, xn, body, 0)

    def gather_pass(panel):
        drain(yr.at[panel, block(facing, piece), :], ap_recv.at[panel])
        gather_send(panel, facing, False)

    def gather_end(panel):
        if xn > 1:
            drain(yr.at[panel, 0:2 * (xn - 1) * piece, :], ag_recv.at[panel])

    def reduced(panel):
        drain(rs.at[panel, 0:(nz - 1) * piece, :], rs_recv.at[panel])
        total = rs[panel, 0:piece, :]
        for other in range(1, nz):
            total = total + rs[panel, other * piece:(other + 1) * piece, :]
        y1[panel, z_rows, :] = total
        yr[panel, mine_rows, :] = total
        spread(y1.at[panel], 2 + panel)
        sp[1 + panel, :size] = exact(nb if panel else na, total, TN)
        sp[1 + panel, size:] = exact(nb, total, TN)
        sum_start(1 + panel)
        gather_send(panel, col, True)

    reduced(0)

    load_f.wait()
    f1, f2 = f_ref[0], f_ref[1]
    va, vb = v_ref[0], v_ref[1]
    sum_end(0)
    gram = sf[0, :size]
    e = exact(f1, exact(gram, f2))

    def keep(high_ref, low_ref, index, value):
        high, low = halves(value)
        high_ref[:, 2 * index * size:(2 * index + 1) * size] = high
        high_ref[:, (2 * index + 1) * size:(2 * index + 2) * size] = high
        low_ref[:, index * size:(index + 1) * size] = low

    keep(lh_a, ll_a, 0, exact(va, f1, NT) - exact(vb, e, NT))
    keep(lh_b, ll_b, 0, exact(vb, f2, NT))

    deliver(y1.at[0], yc.at[0], 2, 0, nz // 2)
    reduced(1)
    deliver(y1.at[0], yc.at[0], 2, nz // 2, nz)
    gather_pass(0)
    sum_level(1)
    deliver(y1.at[1], yc.at[1], 3, 0, nz // 2)
    sum_level(2)
    sum_share(1)
    deliver(y1.at[1], yc.at[1], 3, nz // 2, nz)
    gather_pass(1)
    relay(yc.at[0], 2)
    sum_share(2)
    for side in range(2):
        partner(yc.at[0], 2, side)
    fold(yc.at[0], 0, 0, slice(0, width))
    gather_end(0)
    ya = yr[0]
    sum_end(1)
    s11, s21 = sf[1, :size], sf[1, size:]
    k1 = exact(exact(f1, s11, TN), f1)
    fs = exact(f1, s21, (((0,), (1,)), ((), ())))
    kg = exact(k1, gram)
    mixed = exact(kg - fs, f2)
    gt = exact(gram, fs - 0.5 * kg, TN)
    keep(lh_a, ll_a, 1, exact(ya, f1) - exact(va, k1) + exact(vb, mixed, NT))
    relay(yc.at[1], 3)

    def first_terms(index, carry):
        span = pl.ds(pl.multiple_of(index * tile, tile), tile)
        a_buf[:, span] = a_buf[:, span] - drop(lh_a, ll_a, right_a, span)
        return carry

    lax.fori_loop(0, width // tile, first_terms, 0)
    gather_end(1)
    rest = exact(yr[1], f2) - exact(ya, e) + exact(va, mixed)
    for side in range(2):
        partner(yc.at[1], 3, side)
    fold(yc.at[1], 1, 0, slice(0, width))
    sum_end(2)
    k2 = exact(exact(f2, sf[2, :size] - gt - gt.T, TN), f2)
    keep(lh_b, ll_b, 1, rest - exact(vb, k2))

    for panel in range(2):
        settle(v1.at[panel], vc.at[panel], panel)
        settle(y1.at[panel], yc.at[panel], 2 + panel)
        drain(rs.at[panel, 0:(nz - 1) * piece, :], rs_send.at[panel])
        drain(rs.at[panel, 0:(nz - 1) * piece, :], ag_send.at[panel])
    for group in range(3):
        sum_settle(group)


def apply_update(tile, a_ref, right, lh, ll, out, stage, sems):
    count = out.shape[1] // tile

    def store(slot, index):
        span = pl.ds(pl.multiple_of(index * tile, tile), tile)
        return pltpu.make_async_copy(stage.at[slot], out.at[:, span], sems.at[slot])

    def body(index, carry):
        slot = index % 2

        @pl.when(index >= 2)
        def _():
            store(slot, index - 2).wait()

        span = pl.ds(pl.multiple_of(index * tile, tile), tile)
        stage[slot] = a_ref[:, span] - drop(lh, ll, right, span)
        store(slot, index).start()
        return carry

    lax.fori_loop(0, count, body, 0)
    for index in range(max(count - 2, 0), count):
        store(index % 2, index).wait()


def shards(nz, matrix, panels, factors):
    rows, width = matrix.shape
    size = panels.shape[2]
    srows = 2 * size // (4 * nz)
    tile = 256 if width % 256 == 0 else width
    vmem = pl.BlockSpec(memory_space=pltpu.VMEM)
    hbm = pl.BlockSpec(memory_space=pltpu.HBM)
    block = pltpu.VMEM((2, rows, size), F32)
    wide = pltpu.VMEM((2, width, size), F32)
    sums = pltpu.VMEM((3, 2 * size, size), F32)
    dma = pltpu.SemaphoreType.DMA
    held = pl.pallas_call(
        functools.partial(exchange, nz, tile),
        out_shape=(
            jax.ShapeDtypeStruct(matrix.shape, F32),
            jax.ShapeDtypeStruct((width, 4 * size), BF16),
            jax.ShapeDtypeStruct((rows, 4 * size), BF16),
            jax.ShapeDtypeStruct((rows, 2 * size), BF16),
        ),
        in_specs=[hbm, hbm, hbm],
        out_specs=(vmem,) * 4,
        scratch_shapes=[
            pltpu.VMEM((width, 4 * size), BF16), pltpu.VMEM((rows, 4 * size), BF16),
            pltpu.VMEM((rows, 2 * size), BF16),
            pltpu.VMEM((rows, width), BF16), pltpu.VMEM((rows, width), BF16),
            block, pltpu.VMEM(factors.shape, F32), wide, wide,
            block, block, block, block, block,
            sums, pltpu.VMEM((3, 4 * nz, srows, size), F32),
            pltpu.VMEM((3, nz, srows, size), F32), sums,
            dma(()), dma(()), dma(()), dma(()), dma((4, 5)), dma((4, nz)), dma((4, 2)), dma((4, 2)),
        ] + [dma((2,))] * 5 + [dma((3,))] * 6,
        compiler_params=pltpu.CompilerParams(collective_id=0, has_side_effects=True, vmem_limit_bytes=40 << 20),
        name="exchange",
    )(*(pltpu.with_memory_space_constraint(x, pltpu.HBM) for x in (matrix, panels, factors)))
    return pl.pallas_call(
        functools.partial(apply_update, tile),
        out_shape=jax.ShapeDtypeStruct(matrix.shape, F32),
        in_specs=[vmem] * 4,
        out_specs=hbm,
        scratch_shapes=[pltpu.VMEM((2, rows, tile), F32), dma((2,))],
        compiler_params=pltpu.CompilerParams(vmem_limit_bytes=24 << 20),
        name="apply_update",
    )(*held)


def solution(mesh):
    placed = (P("row", "col"), P(None, "row", None), P())
    return jax.shard_map(
        functools.partial(shards, mesh.shape["col"]),
        mesh=mesh, in_specs=placed, out_specs=P("row", "col"), check_vma=False,
    )
```

```python
import functools

import jax
import jax.numpy as jnp
from jax import lax
from jax.experimental import pallas as pl
from jax.experimental.pallas import tpu as pltpu
from jax.sharding import PartitionSpec as P

MESH = pl.DeviceIdType.MESH
F32 = jnp.float32
BF16 = jnp.bfloat16
NN = (((1,), (0,)), ((), ()))
NT = (((1,), (1,)), ((), ()))
TN = (((0,), (0,)), ((), ()))


def exact(a, b, dims=NN):
    return lax.dot_general(
        a, b, dims, precision=lax.Precision.HIGHEST, preferred_element_type=F32
    )


def halves(value):
    high = value.astype(BF16)
    return high, (value - high.astype(F32)).astype(BF16)


def drop(left, low, right, span):
    size = right.shape[1] // 4
    highs = jnp.concatenate([right[span, 0:size], right[span, 2 * size:3 * size]], axis=1)
    value = lax.dot_general(low[...], highs, NT, preferred_element_type=F32)
    return value + lax.dot_general(left[...], right[span, :], NT, preferred_element_type=F32)


def exchange(nz, tile, a_hbm, v_hbm, f_hbm, a_buf, right_b, lh_b, ll_b,
             right_a, lh_a, ll_a, ah, al, v_ref, f_ref, vc, yc, v1, p_buf, rs, y1, yr, sp, srs, szs, sf,
             a_sem, v_sem, f_sem, own_sem, g_send, g1_recv, g2_recv, g3_recv,
             rs_send, rs_recv, ag_send, ag_recv, ap_recv, ss_send, ss_recv, sg_send, sg_recv, sz_send, sz_recv):
    row, col = lax.axis_index("row"), lax.axis_index("col")
    z, quad = row // 4, row % 4
    yl, core = quad // 2, quad % 2
    rows, width = a_buf.shape
    size = v_ref.shape[2]
    piece = rows // nz
    plane = 4 * nz
    srows = sp.shape[1] // plane
    mine = col * 4 + quad

    def block(index, step):
        return pl.ds(pl.multiple_of(index * step, 8), step)

    def send(src, dst, ssem, rsem, to_row, to_col):
        pltpu.make_async_remote_copy(
            src_ref=src, dst_ref=dst, send_sem=ssem, recv_sem=rsem,
            device_id=(to_row, to_col), device_id_type=MESH,
        ).start()

    def drain(ref, sem):
        pltpu.make_async_copy(ref, ref, sem).wait()

    load_v = pltpu.make_async_copy(v_hbm, v_ref, v_sem)
    load_v.start()
    load_f = pltpu.make_async_copy(f_hbm, f_ref, f_sem)
    load_f.start()
    load = pltpu.make_async_copy(a_hbm, a_buf, a_sem)
    load.start()
    mine_rows, z_rows, s_rows = block(col, piece), block(z, piece), block(mine, srows)
    own = pltpu.make_async_copy(v_ref.at[:, mine_rows, :], v1.at[:, z_rows, :], own_sem)

    def zpeer(step):
        return (z + step) % nz

    def ppeer(step):
        other = (mine + step) % plane
        return z * 4 + other % 4, other // 4

    barrier = pltpu.get_barrier_semaphore()

    def greet_z(step, carry):
        pl.semaphore_signal(barrier, inc=1, device_id=(zpeer(step) * 4 + quad, col), device_id_type=MESH)
        return carry

    def greet_plane(step, carry):
        pl.semaphore_signal(barrier, inc=1, device_id=ppeer(step), device_id_type=MESH)
        return carry

    lax.fori_loop(1, nz, greet_z, 0)
    lax.fori_loop(1, plane, greet_plane, 0)
    load_v.wait()
    own.start()
    own.wait()
    pl.semaphore_wait(barrier, nz - 1 + plane - 1)

    turn = col + 4 * core

    def hop(index):
        return (index + turn) % nz

    def spread_one(held, which, index):
        part = held.at[z_rows, :]
        to = (z + hop(index)) % nz

        @pl.when(to != z)
        def _():
            send(part, part, g_send.at[which, 0], g1_recv.at[which, z], to * 4 + quad, col)

    def spread(held, which):
        def body(index, carry):
            spread_one(held, which, index)
            return carry

        lax.fori_loop(0, nz, body, 0)

    def hand_on(held, full, which, target):
        src = held.at[block(target, piece), :]
        dst = full.at[pl.ds(pl.multiple_of(quad * rows + col * piece, 8), piece), :]
        send(src, dst, g_send.at[which, 1], g2_recv.at[which, yl], z * 4 + (1 - yl) * 2 + core, target)

        @pl.when(target != col)
        def _():
            send(src, dst, g_send.at[which, 2], g2_recv.at[which, yl], row, target)

        @pl.when(target == col)
        def _():
            pltpu.make_async_copy(src, dst, g2_recv.at[which, yl]).start()

    def deliver(held, full, which, first, last, following=None):
        def body(index, carry):
            target = (z + nz - hop(index)) % nz

            @pl.when(target != z)
            def _():
                drain(held.at[block(target, piece), :], g1_recv.at[which, target])

            hand_on(held, full, which, target)
            if following is not None:
                spread_one(following, which + 1, index)
            return carry

        lax.fori_loop(first, last, body, 0)

    def relay(full, which):
        for side in range(2):
            part = full.at[block(side * 2 + core, rows), :]
            drain(part, g2_recv.at[which, side])
            send(part, part, g_send.at[which, 3 + side], g3_recv.at[which, side], z * 4 + yl * 2 + (1 - core), col)

    def partner(full, which, side):
        drain(full.at[block(side * 2 + (1 - core), rows), :], g3_recv.at[which, side])

    def settle(held, full, which):
        drain(held.at[0:(nz - 1) * piece, :], g_send.at[which, 0])
        drain(held.at[0:nz * piece, :], g_send.at[which, 1])
        drain(held.at[0:(nz - 1) * piece, :], g_send.at[which, 2])
        for side in range(2):
            drain(full.at[0:rows, :], g_send.at[which, 3 + side])

    def sum_start(group):
        def body(step, carry):
            to_row, to_col = ppeer(step)
            other = (mine + step) % plane
            send(sp.at[group, block(other, srows), :], srs.at[group, mine], ss_send.at[group], ss_recv.at[group], to_row, to_col)
            return carry

        lax.fori_loop(1, plane, body, 0)
        srs[group, mine] = sp[group, s_rows, :]

    def sum_level(group):
        drain(srs.at[group, 0:plane - 1], ss_recv.at[group])
        szs[group, z] = jnp.sum(srs[group], axis=0)

        def body(step, carry):
            part = szs.at[group, z]
            send(part, part, sz_send.at[group], sz_recv.at[group], zpeer(step) * 4 + quad, col)
            return carry

        lax.fori_loop(1, nz, body, 0)

    def sum_share(group):
        drain(szs.at[group, 0:nz - 1], sz_recv.at[group])
        sf[group, s_rows, :] = jnp.sum(szs[group], axis=0)

        def body(step, carry):
            to_row, to_col = ppeer(step)
            part = sf.at[group, s_rows, :]
            send(part, part, sg_send.at[group], sg_recv.at[group], to_row, to_col)
            return carry

        lax.fori_loop(1, plane, body, 0)

    def sum_end(group):
        drain(sf.at[group, 0:(plane - 1) * srows, :], sg_recv.at[group])

    def sum_settle(group):
        drain(srs.at[group, 0:plane - 1], ss_send.at[group])
        drain(szs.at[group, 0:nz - 1], sz_send.at[group])
        drain(srs.at[group, 0:plane - 1], sg_send.at[group])

    spread(v1.at[0], 0)
    na, nb = v_ref[0, mine_rows, :], v_ref[1, mine_rows, :]
    sp[0, :size] = exact(na, nb, TN)
    sp[0, size:] = sp[0, :size]
    sum_start(0)
    load.wait()
    ah[...], al[...] = halves(a_buf[...])
    deliver(v1.at[0], vc.at[0], 0, 0, nz, v1.at[1])
    deliver(v1.at[1], vc.at[1], 1, 0, nz // 2)
    relay(vc.at[0], 0)
    deliver(v1.at[1], vc.at[1], 1, nz // 2, nz)
    sum_level(0)

    rights = (right_a, right_b)

    def fold(full, panel, base, span):
        high, low = halves(full[span, :])
        rights[panel][span, base:base + size] = high
        rights[panel][span, base + size:base + 2 * size] = low

    for panel in range(2):
        if panel:
            relay(vc.at[1], 1)
            sum_share(0)
        held = rights[panel]
        for side in range(2):
            partner(vc.at[panel], panel, side)
            span = slice(side * 2 * rows, (side + 1) * 2 * rows)
            fold(vc.at[panel], panel, 2 * size, span)
            both = lax.dot_general(ah[:, span], held[span, 2 * size:], NN, preferred_element_type=F32)
            part = lax.dot_general(al[:, span], held[span, 2 * size:3 * size], NN, preferred_element_type=F32)
            part = part + both[:, size:] + both[:, :size]
            p_buf[panel] = part if side == 0 else p_buf[panel] + part

        def scatter(step, carry, panel=panel):
            to = (col + step) % nz
            send(p_buf.at[panel, block(to, piece), :], rs.at[panel, mine_rows, :], rs_send.at[panel], rs_recv.at[panel], row, to)
            return carry

        lax.fori_loop(1, nz, scatter, 0)
        rs[panel, mine_rows, :] = p_buf[panel, mine_rows, :]

    xn = nz // 2
    facing = (col + xn) % nz

    def gather_send(panel, owner, with_facing):
        part = yr.at[panel, block(owner, piece), :]
        if with_facing:
            send(part, part, ag_send.at[panel], ap_recv.at[panel], row, facing)

        def body(step, carry):
            to = (col // xn) * xn + (col + step) % xn
            send(part, part, ag_send.at[panel], ag_recv.at[panel], row, to)
            return carry

        lax.fori_loop(1, xn, body, 0)

    def gather_pass(panel):
        drain(yr.at[panel, block(facing, piece), :], ap_recv.at[panel])
        gather_send(panel, facing, False)

    def gather_end(panel):
        if xn > 1:
            drain(yr.at[panel, 0:2 * (xn - 1) * piece, :], ag_recv.at[panel])

    def reduced(panel):
        drain(rs.at[panel, 0:(nz - 1) * piece, :], rs_recv.at[panel])
        total = rs[panel, 0:piece, :]
        for other in range(1, nz):
            total = total + rs[panel, other * piece:(other + 1) * piece, :]
        y1[panel, z_rows, :] = total
        yr[panel, mine_rows, :] = total
        spread(y1.at[panel], 2 + panel)
        sp[1 + panel, :size] = exact(nb if panel else na, total, TN)
        sp[1 + panel, size:] = exact(nb, total, TN)
        sum_start(1 + panel)
        gather_send(panel, col, True)

    reduced(0)

    load_f.wait()
    f1, f2 = f_ref[0], f_ref[1]
    va, vb = v_ref[0], v_ref[1]
    sum_end(0)
    gram = sf[0, :size]
    e = exact(f1, exact(gram, f2))

    def keep(high_ref, low_ref, index, value):
        high, low = halves(value)
        high_ref[:, 2 * index * size:(2 * index + 1) * size] = high
        high_ref[:, (2 * index + 1) * size:(2 * index + 2) * size] = high
        low_ref[:, index * size:(index + 1) * size] = low

    keep(lh_a, ll_a, 0, exact(va, f1, NT) - exact(vb, e, NT))
    keep(lh_b, ll_b, 0, exact(vb, f2, NT))

    deliver(y1.at[0], yc.at[0], 2, 0, nz // 2)
    sum_level(1)
    reduced(1)
    deliver(y1.at[0], yc.at[0], 2, nz // 2, nz)
    gather_pass(0)
    sum_share(1)
    deliver(y1.at[1], yc.at[1], 3, 0, nz // 2)
    sum_level(2)
    deliver(y1.at[1], yc.at[1], 3, nz // 2, nz)
    relay(yc.at[0], 2)
    gather_end(0)
    ya = yr[0]
    most = exact(ya, f1)
    crossed = exact(ya, e)
    sum_share(2)
    gather_pass(1)
    for side in range(2):
        partner(yc.at[0], 2, side)
    fold(yc.at[0], 0, 0, slice(0, width))
    sum_end(1)
    s11, s21 = sf[1, :size], sf[1, size:]
    k1 = exact(exact(f1, s11, TN), f1)
    fs = exact(f1, s21, (((0,), (1,)), ((), ())))
    kg = exact(k1, gram)
    mixed = exact(kg - fs, f2)
    gt = exact(gram, fs - 0.5 * kg, TN)
    keep(lh_a, ll_a, 1, most - exact(va, k1) + exact(vb, mixed, NT))

    def first_terms(index, carry):
        span = pl.ds(pl.multiple_of(index * tile, tile), tile)
        a_buf[:, span] = a_buf[:, span] - drop(lh_a, ll_a, right_a, span)
        return carry

    lax.fori_loop(0, width // tile, first_terms, 0)
    relay(yc.at[1], 3)
    gather_end(1)
    rest = exact(yr[1], f2) - crossed + exact(va, mixed)
    for side in range(2):
        partner(yc.at[1], 3, side)
    fold(yc.at[1], 1, 0, slice(0, width))
    sum_end(2)
    k2 = exact(exact(f2, sf[2, :size] - gt - gt.T, TN), f2)
    keep(lh_b, ll_b, 1, rest - exact(vb, k2))

    for panel in range(2):
        settle(v1.at[panel], vc.at[panel], panel)
        settle(y1.at[panel], yc.at[panel], 2 + panel)
        drain(rs.at[panel, 0:(nz - 1) * piece, :], rs_send.at[panel])
        drain(rs.at[panel, 0:(nz - 1) * piece, :], ag_send.at[panel])
    for group in range(3):
        sum_settle(group)


def apply_update(tile, a_ref, right, lh, ll, out, stage, sems):
    count = out.shape[1] // tile

    def store(slot, index):
        span = pl.ds(pl.multiple_of(index * tile, tile), tile)
        return pltpu.make_async_copy(stage.at[slot], out.at[:, span], sems.at[slot])

    def body(index, carry):
        slot = index % 2

        @pl.when(index >= 2)
        def _():
            store(slot, index - 2).wait()

        span = pl.ds(pl.multiple_of(index * tile, tile), tile)
        stage[slot] = a_ref[:, span] - drop(lh, ll, right, span)
        store(slot, index).start()
        return carry

    lax.fori_loop(0, count, body, 0)
    for index in range(max(count - 2, 0), count):
        store(index % 2, index).wait()


def shards(nz, matrix, panels, factors):
    rows, width = matrix.shape
    size = panels.shape[2]
    srows = 2 * size // (4 * nz)
    tile = 256 if width % 256 == 0 else width
    vmem = pl.BlockSpec(memory_space=pltpu.VMEM)
    hbm = pl.BlockSpec(memory_space=pltpu.HBM)
    block = pltpu.VMEM((2, rows, size), F32)
    wide = pltpu.VMEM((2, width, size), F32)
    sums = pltpu.VMEM((3, 2 * size, size), F32)
    dma = pltpu.SemaphoreType.DMA
    held = pl.pallas_call(
        functools.partial(exchange, nz, tile),
        out_shape=(
            jax.ShapeDtypeStruct(matrix.shape, F32),
            jax.ShapeDtypeStruct((width, 4 * size), BF16),
            jax.ShapeDtypeStruct((rows, 4 * size), BF16),
            jax.ShapeDtypeStruct((rows, 2 * size), BF16),
        ),
        in_specs=[hbm, hbm, hbm],
        out_specs=(vmem,) * 4,
        scratch_shapes=[
            pltpu.VMEM((width, 4 * size), BF16), pltpu.VMEM((rows, 4 * size), BF16),
            pltpu.VMEM((rows, 2 * size), BF16),
            pltpu.VMEM((rows, width), BF16), pltpu.VMEM((rows, width), BF16),
            block, pltpu.VMEM(factors.shape, F32), wide, wide,
            block, block, block, block, block,
            sums, pltpu.VMEM((3, 4 * nz, srows, size), F32),
            pltpu.VMEM((3, nz, srows, size), F32), sums,
            dma(()), dma(()), dma(()), dma(()), dma((4, 5)), dma((4, nz)), dma((4, 2)), dma((4, 2)),
        ] + [dma((2,))] * 5 + [dma((3,))] * 6,
        compiler_params=pltpu.CompilerParams(collective_id=0, has_side_effects=True, vmem_limit_bytes=40 << 20),
        name="exchange",
    )(*(pltpu.with_memory_space_constraint(x, pltpu.HBM) for x in (matrix, panels, factors)))
    return pl.pallas_call(
        functools.partial(apply_update, tile),
        out_shape=jax.ShapeDtypeStruct(matrix.shape, F32),
        in_specs=[vmem] * 4,
        out_specs=hbm,
        scratch_shapes=[pltpu.VMEM((2, rows, tile), F32), dma((2,))],
        compiler_params=pltpu.CompilerParams(vmem_limit_bytes=24 << 20),
        name="apply_update",
    )(*held)


def solution(mesh):
    placed = (P("row", "col"), P(None, "row", None), P())
    return jax.shard_map(
        functools.partial(shards, mesh.shape["col"]),
        mesh=mesh, in_specs=placed, out_specs=P("row", "col"), check_vma=False,
    )
```

```python
import functools

import jax
import jax.numpy as jnp
from jax import lax
from jax.experimental import pallas as pl
from jax.experimental.pallas import tpu as pltpu
from jax.sharding import PartitionSpec as P

MESH = pl.DeviceIdType.MESH
F32 = jnp.float32
BF16 = jnp.bfloat16
NN = (((1,), (0,)), ((), ()))
NT = (((1,), (1,)), ((), ()))
TN = (((0,), (0,)), ((), ()))


def exact(a, b, dims=NN):
    return lax.dot_general(
        a, b, dims, precision=lax.Precision.HIGHEST, preferred_element_type=F32
    )


def halves(value):
    high = value.astype(BF16)
    return high, (value - high.astype(F32)).astype(BF16)


def drop(left, low, right, span):
    size = right.shape[1] // 4
    highs = jnp.concatenate([right[span, 0:size], right[span, 2 * size:3 * size]], axis=1)
    value = lax.dot_general(low[...], highs, NT, preferred_element_type=F32)
    return value + lax.dot_general(left[...], right[span, :], NT, preferred_element_type=F32)


def exchange(nz, tile, a_hbm, v_hbm, f_hbm, a_buf, right_b, lh_b, ll_b,
             right_a, lh_a, ll_a, ah, al, v_ref, f_ref, vc, yc, v1, p_buf, rs, y1, yr, sp, srs, szs, sf,
             a_sem, v_sem, f_sem, own_sem, g_send, g1_recv, g2_recv, g3_recv,
             rs_send, rs_recv, ag_send, ag_recv, ap_recv, ss_send, ss_recv, sg_send, sg_recv, sz_send, sz_recv):
    row, col = lax.axis_index("row"), lax.axis_index("col")
    z, quad = row // 4, row % 4
    yl, core = quad // 2, quad % 2
    rows, width = a_buf.shape
    size = v_ref.shape[2]
    piece = rows // nz
    plane = 4 * nz
    srows = sp.shape[1] // plane
    mine = col * 4 + quad

    def block(index, step):
        return pl.ds(pl.multiple_of(index * step, 8), step)

    def send(src, dst, ssem, rsem, to_row, to_col):
        pltpu.make_async_remote_copy(
            src_ref=src, dst_ref=dst, send_sem=ssem, recv_sem=rsem,
            device_id=(to_row, to_col), device_id_type=MESH,
        ).start()

    def drain(ref, sem):
        pltpu.make_async_copy(ref, ref, sem).wait()

    load_v = pltpu.make_async_copy(v_hbm, v_ref, v_sem)
    load_v.start()
    load_f = pltpu.make_async_copy(f_hbm, f_ref, f_sem)
    load_f.start()
    load = pltpu.make_async_copy(a_hbm, a_buf, a_sem)
    load.start()
    mine_rows, z_rows, s_rows = block(col, piece), block(z, piece), block(mine, srows)
    own = pltpu.make_async_copy(v_ref.at[:, mine_rows, :], v1.at[:, z_rows, :], own_sem)

    def zpeer(step):
        return (z + step) % nz

    def ppeer(step):
        other = (mine + step) % plane
        return z * 4 + other % 4, other // 4

    barrier = pltpu.get_barrier_semaphore()

    def greet_z(step, carry):
        pl.semaphore_signal(barrier, inc=1, device_id=(zpeer(step) * 4 + quad, col), device_id_type=MESH)
        return carry

    def greet_plane(step, carry):
        pl.semaphore_signal(barrier, inc=1, device_id=ppeer(step), device_id_type=MESH)
        return carry

    lax.fori_loop(1, nz, greet_z, 0)
    lax.fori_loop(1, plane, greet_plane, 0)
    load_v.wait()
    own.start()
    own.wait()
    pl.semaphore_wait(barrier, nz - 1 + plane - 1)

    turn = col + 4 * core

    def hop(index):
        return (index + turn) % nz

    def spread_one(held, which, index):
        part = held.at[z_rows, :]
        to = (z + hop(index)) % nz

        @pl.when(to != z)
        def _():
            send(part, part, g_send.at[which, 0], g1_recv.at[which, z], to * 4 + quad, col)

    def spread(held, which):
        def body(index, carry):
            spread_one(held, which, index)
            return carry

        lax.fori_loop(0, nz, body, 0)

    def hand_on(held, full, which, target):
        src = held.at[block(target, piece), :]
        dst = full.at[pl.ds(pl.multiple_of(quad * rows + col * piece, 8), piece), :]
        send(src, dst, g_send.at[which, 1], g2_recv.at[which, yl], z * 4 + (1 - yl) * 2 + core, target)

        @pl.when(target != col)
        def _():
            send(src, dst, g_send.at[which, 2], g2_recv.at[which, yl], row, target)

        @pl.when(target == col)
        def _():
            pltpu.make_async_copy(src, dst, g2_recv.at[which, yl]).start()

    def deliver(held, full, which, first, last, following=None):
        def body(index, carry):
            target = (z + nz - hop(index)) % nz

            @pl.when(target != z)
            def _():
                drain(held.at[block(target, piece), :], g1_recv.at[which, target])

            hand_on(held, full, which, target)
            if following is not None:
                spread_one(following, which + 1, index)
            return carry

        lax.fori_loop(first, last, body, 0)

    def relay(full, which):
        for side in range(2):
            part = full.at[block(side * 2 + core, rows), :]
            drain(part, g2_recv.at[which, side])
            send(part, part, g_send.at[which, 3 + side], g3_recv.at[which, side], z * 4 + yl * 2 + (1 - core), col)

    def partner(full, which, side):
        drain(full.at[block(side * 2 + (1 - core), rows), :], g3_recv.at[which, side])

    def settle(held, full, which):
        drain(held.at[0:(nz - 1) * piece, :], g_send.at[which, 0])
        drain(held.at[0:nz * piece, :], g_send.at[which, 1])
        drain(held.at[0:(nz - 1) * piece, :], g_send.at[which, 2])
        for side in range(2):
            drain(full.at[0:rows, :], g_send.at[which, 3 + side])

    def own_rows(group):
        return s_rows if group == 1 else block(mine // 2, srows)

    def if_owner(group):
        return pl.when(core == 0) if group != 1 else (lambda body: body())

    def sum_start(group):
        if group == 1:
            def body(step, carry):
                to_row, to_col = ppeer(step)
                other = (mine + step) % plane
                send(sp.at[group, block(other, srows), :], srs.at[group, mine], ss_send.at[group], ss_recv.at[group], to_row, to_col)
                return carry

            lax.fori_loop(1, plane, body, 0)
        else:
            def body(step, carry):
                owner = (mine // 2 + step) % (plane // 2)

                @pl.when((step > 0) | (core == 1))
                def _():
                    send(sp.at[group, block(owner, srows), :], srs.at[group, mine], ss_send.at[group], ss_recv.at[group], z * 4 + (owner % 2) * 2, owner // 2)

                return carry

            lax.fori_loop(0, plane // 2, body, 0)

        @if_owner(group)
        def _():
            srs[group, mine] = sp[group, own_rows(group), :]

    def sum_level(group):
        @if_owner(group)
        def _():
            drain(srs.at[group, 0:plane - 1], ss_recv.at[group])
            szs[group, z] = jnp.sum(srs[group], axis=0)

            def body(step, carry):
                part = szs.at[group, z]
                send(part, part, sz_send.at[group], sz_recv.at[group], zpeer(step) * 4 + quad, col)
                return carry

            lax.fori_loop(1, nz, body, 0)

    def sum_share(group):
        @if_owner(group)
        def _():
            drain(szs.at[group, 0:nz - 1], sz_recv.at[group])
            sf[group, own_rows(group), :] = jnp.sum(szs[group], axis=0)

            def body(step, carry):
                to_row, to_col = ppeer(step)
                part = sf.at[group, own_rows(group), :]
                send(part, part, sg_send.at[group], sg_recv.at[group], to_row, to_col)
                return carry

            lax.fori_loop(1, plane, body, 0)

    def drain_others(ref, sem):
        for parity in range(2):
            @pl.when(core == parity)
            def _(parity=parity):
                drain(ref.at[0:(plane // 2 - 1 + parity) * srows, :], sem)

    def sum_end(group):
        if group == 1:
            drain(sf.at[group, 0:(plane - 1) * srows, :], sg_recv.at[group])
        else:
            drain_others(sf.at[group], sg_recv.at[group])

    def sum_settle(group):
        if group == 1:
            drain(srs.at[group, 0:plane - 1], ss_send.at[group])
        else:
            drain_others(sf.at[group], ss_send.at[group])

        @if_owner(group)
        def _():
            drain(szs.at[group, 0:nz - 1], sz_send.at[group])
            drain(srs.at[group, 0:plane - 1], sg_send.at[group])

    spread(v1.at[0], 0)
    na, nb = v_ref[0, mine_rows, :], v_ref[1, mine_rows, :]
    sp[0, :size] = exact(na, nb, TN)
    sum_start(0)
    load.wait()
    ah[...], al[...] = halves(a_buf[...])
    deliver(v1.at[0], vc.at[0], 0, 0, nz, v1.at[1])
    deliver(v1.at[1], vc.at[1], 1, 0, nz // 2)
    relay(vc.at[0], 0)
    deliver(v1.at[1], vc.at[1], 1, nz // 2, nz)
    sum_level(0)

    rights = (right_a, right_b)

    def fold(full, panel, base, span):
        high, low = halves(full[span, :])
        rights[panel][span, base:base + size] = high
        rights[panel][span, base + size:base + 2 * size] = low

    for panel in range(2):
        if panel:
            relay(vc.at[1], 1)
            sum_share(0)
        held = rights[panel]
        for side in range(2):
            partner(vc.at[panel], panel, side)
            span = slice(side * 2 * rows, (side + 1) * 2 * rows)
            fold(vc.at[panel], panel, 2 * size, span)
            both = lax.dot_general(ah[:, span], held[span, 2 * size:], NN, preferred_element_type=F32)
            part = lax.dot_general(al[:, span], held[span, 2 * size:3 * size], NN, preferred_element_type=F32)
            part = part + both[:, size:] + both[:, :size]
            p_buf[panel] = part if side == 0 else p_buf[panel] + part

        def scatter(step, carry, panel=panel):
            to = (col + step) % nz
            send(p_buf.at[panel, block(to, piece), :], rs.at[panel, mine_rows, :], rs_send.at[panel], rs_recv.at[panel], row, to)
            return carry

        lax.fori_loop(1, nz, scatter, 0)
        rs[panel, mine_rows, :] = p_buf[panel, mine_rows, :]

    xn = nz // 2
    facing = (col + xn) % nz

    def gather_send(panel, owner, with_facing):
        part = yr.at[panel, block(owner, piece), :]
        if with_facing:
            send(part, part, ag_send.at[panel], ap_recv.at[panel], row, facing)

        def body(step, carry):
            to = (col // xn) * xn + (col + step) % xn
            send(part, part, ag_send.at[panel], ag_recv.at[panel], row, to)
            return carry

        lax.fori_loop(1, xn, body, 0)

    def gather_pass(panel):
        drain(yr.at[panel, block(facing, piece), :], ap_recv.at[panel])
        gather_send(panel, facing, False)

    def gather_end(panel):
        if xn > 1:
            drain(yr.at[panel, 0:2 * (xn - 1) * piece, :], ag_recv.at[panel])

    def reduced(panel):
        drain(rs.at[panel, 0:(nz - 1) * piece, :], rs_recv.at[panel])
        total = rs[panel, 0:piece, :]
        for other in range(1, nz):
            total = total + rs[panel, other * piece:(other + 1) * piece, :]
        y1[panel, z_rows, :] = total
        yr[panel, mine_rows, :] = total
        spread(y1.at[panel], 2 + panel)
        sp[1 + panel, :size] = exact(nb if panel else na, total, TN)
        if panel == 0:
            sp[1, size:] = exact(nb, total, TN)
        sum_start(1 + panel)
        gather_send(panel, col, True)

    reduced(0)

    load_f.wait()
    f1, f2 = f_ref[0], f_ref[1]
    va, vb = v_ref[0], v_ref[1]
    sum_end(0)
    gram = sf[0, :size]
    e = exact(f1, exact(gram, f2))

    def keep(high_ref, low_ref, index, value):
        high, low = halves(value)
        high_ref[:, 2 * index * size:(2 * index + 1) * size] = high
        high_ref[:, (2 * index + 1) * size:(2 * index + 2) * size] = high
        low_ref[:, index * size:(index + 1) * size] = low

    keep(lh_a, ll_a, 0, exact(va, f1, NT) - exact(vb, e, NT))
    keep(lh_b, ll_b, 0, exact(vb, f2, NT))

    deliver(y1.at[0], yc.at[0], 2, 0, nz // 2)
    sum_level(1)
    reduced(1)
    deliver(y1.at[0], yc.at[0], 2, nz // 2, nz)
    gather_pass(0)
    sum_share(1)
    deliver(y1.at[1], yc.at[1], 3, 0, nz // 2)
    sum_level(2)
    deliver(y1.at[1], yc.at[1], 3, nz // 2, nz)
    relay(yc.at[0], 2)
    gather_end(0)
    ya = yr[0]
    most = exact(ya, f1)
    crossed = exact(ya, e)
    sum_share(2)
    gather_pass(1)
    for side in range(2):
        partner(yc.at[0], 2, side)
    fold(yc.at[0], 0, 0, slice(0, width))
    sum_end(1)
    s11, s21 = sf[1, :size], sf[1, size:]
    k1 = exact(exact(f1, s11, TN), f1)
    fs = exact(f1, s21, (((0,), (1,)), ((), ())))
    kg = exact(k1, gram)
    mixed = exact(kg - fs, f2)
    gt = exact(gram, fs - 0.5 * kg, TN)
    keep(lh_a, ll_a, 1, most - exact(va, k1) + exact(vb, mixed, NT))

    def first_terms(index, carry):
        span = pl.ds(pl.multiple_of(index * tile, tile), tile)
        a_buf[:, span] = a_buf[:, span] - drop(lh_a, ll_a, right_a, span)
        return carry

    for index in range(0, width, 256):
        span = slice(index, index + 256)
        a_buf[:, span] = a_buf[:, span] - drop(lh_a, ll_a, right_a, span)
    relay(yc.at[1], 3)
    gather_end(1)
    rest = exact(yr[1], f2) - crossed + exact(va, mixed)
    for side in range(2):
        partner(yc.at[1], 3, side)
    fold(yc.at[1], 1, 0, slice(0, width))
    sum_end(2)
    k2 = exact(exact(f2, sf[2, :size] - gt - gt.T, TN), f2)
    keep(lh_b, ll_b, 1, rest - exact(vb, k2))

    for panel in range(2):
        settle(v1.at[panel], vc.at[panel], panel)
        settle(y1.at[panel], yc.at[panel], 2 + panel)
        drain(rs.at[panel, 0:(nz - 1) * piece, :], rs_send.at[panel])
        drain(rs.at[panel, 0:(nz - 1) * piece, :], ag_send.at[panel])
    for group in range(3):
        sum_settle(group)


def apply_update(tile, a_ref, right, lh, ll, out, stage, sems):
    width = out.shape[1]
    ends = list(range(512, width, 512))
    stores = []
    for index, (start, stop) in enumerate(zip([0] + ends, ends + [width])):
        span = slice(start, stop)
        stage[:, span] = a_ref[:, span] - drop(lh, ll, right, span)
        stores.append(pltpu.make_async_copy(stage.at[:, span], out.at[:, span], sems.at[index]))
        stores[-1].start()
    for store in stores:
        store.wait()


def shards(nz, matrix, panels, factors):
    rows, width = matrix.shape
    size = panels.shape[2]
    srows = 2 * size // (4 * nz)
    tile = 896 if width % 896 == 0 else width
    vmem = pl.BlockSpec(memory_space=pltpu.VMEM)
    hbm = pl.BlockSpec(memory_space=pltpu.HBM)
    block = pltpu.VMEM((2, rows, size), F32)
    wide = pltpu.VMEM((2, width, size), F32)
    sums = pltpu.VMEM((3, 2 * size, size), F32)
    dma = pltpu.SemaphoreType.DMA
    held = pl.pallas_call(
        functools.partial(exchange, nz, tile),
        out_shape=(
            jax.ShapeDtypeStruct(matrix.shape, F32),
            jax.ShapeDtypeStruct((width, 4 * size), BF16),
            jax.ShapeDtypeStruct((rows, 4 * size), BF16),
            jax.ShapeDtypeStruct((rows, 2 * size), BF16),
        ),
        in_specs=[hbm, hbm, hbm],
        out_specs=(vmem,) * 4,
        scratch_shapes=[
            pltpu.VMEM((width, 4 * size), BF16), pltpu.VMEM((rows, 4 * size), BF16),
            pltpu.VMEM((rows, 2 * size), BF16),
            pltpu.VMEM((rows, width), BF16), pltpu.VMEM((rows, width), BF16),
            block, pltpu.VMEM(factors.shape, F32), wide, wide,
            block, block, block, block, block,
            sums, pltpu.VMEM((3, 4 * nz, srows, size), F32),
            pltpu.VMEM((3, nz, srows, size), F32), sums,
            dma(()), dma(()), dma(()), dma(()), dma((4, 5)), dma((4, nz)), dma((4, 2)), dma((4, 2)),
        ] + [dma((2,))] * 5 + [dma((3,))] * 6,
        compiler_params=pltpu.CompilerParams(collective_id=0, has_side_effects=True, vmem_limit_bytes=40 << 20),
        name="exchange",
    )(*(pltpu.with_memory_space_constraint(x, pltpu.HBM) for x in (matrix, panels, factors)))
    return pl.pallas_call(
        functools.partial(apply_update, tile),
        out_shape=jax.ShapeDtypeStruct(matrix.shape, F32),
        in_specs=[vmem] * 4,
        out_specs=hbm,
        scratch_shapes=[pltpu.VMEM((rows, width), F32), dma((8,))],
        compiler_params=pltpu.CompilerParams(vmem_limit_bytes=24 << 20),
        name="apply_update",
    )(*held)


def solution(mesh):
    placed = (P("row", "col"), P(None, "row", None), P())
    return jax.shard_map(
        functools.partial(shards, mesh.shape["col"]),
        mesh=mesh, in_specs=placed, out_specs=P("row", "col"), check_vma=False,
    )
```

```python
import functools

import jax
import jax.numpy as jnp
from jax import lax
from jax.experimental import pallas as pl
from jax.experimental.pallas import tpu as pltpu
from jax.sharding import PartitionSpec as P

MESH = pl.DeviceIdType.MESH
F32 = jnp.float32
BF16 = jnp.bfloat16
NN = (((1,), (0,)), ((), ()))
NT = (((1,), (1,)), ((), ()))
TN = (((0,), (0,)), ((), ()))


def exact(a, b, dims=NN):
    return lax.dot_general(
        a, b, dims, precision=lax.Precision.HIGHEST, preferred_element_type=F32
    )


def halves(value):
    high = value.astype(BF16)
    return high, (value - high.astype(F32)).astype(BF16)


def drop(left, low, right, span):
    size = right.shape[1] // 4
    highs = jnp.concatenate([right[span, 0:size], right[span, 2 * size:3 * size]], axis=1)
    value = lax.dot_general(low[...], highs, NT, preferred_element_type=F32)
    return value + lax.dot_general(left[...], right[span, :], NT, preferred_element_type=F32)


def exchange(nz, tile, a_hbm, v_hbm, f_hbm, a_buf, right_b, lh_b, ll_b,
             right_a, lh_a, ll_a, ah, al, v_ref, f_ref, vc, yc, v1, p_buf, rs, y1, yr, sp, srs, szs, sf,
             a_sem, v_sem, f_sem, own_sem, g_send, g1_recv, g2_recv, g3_recv,
             rs_send, rs_recv, ag_send, ag_recv, ap_recv, ss_send, ss_recv, sg_send, sg_recv, sz_send, sz_recv):
    row, col = lax.axis_index("row"), lax.axis_index("col")
    z, quad = row // 4, row % 4
    yl, core = quad // 2, quad % 2
    rows, width = a_buf.shape
    size = v_ref.shape[2]
    piece = rows // nz
    plane = 4 * nz
    srows = sp.shape[1] // plane
    mine = col * 4 + quad

    def block(index, step):
        return pl.ds(pl.multiple_of(index * step, 8), step)

    def send(src, dst, ssem, rsem, to_row, to_col):
        pltpu.make_async_remote_copy(
            src_ref=src, dst_ref=dst, send_sem=ssem, recv_sem=rsem,
            device_id=(to_row, to_col), device_id_type=MESH,
        ).start()

    def drain(ref, sem):
        pltpu.make_async_copy(ref, ref, sem).wait()

    load_v = pltpu.make_async_copy(v_hbm, v_ref, v_sem)
    load_v.start()
    load_f = pltpu.make_async_copy(f_hbm, f_ref, f_sem)
    load_f.start()
    load = pltpu.make_async_copy(a_hbm, a_buf, a_sem)
    load.start()
    mine_rows, z_rows, s_rows = block(col, piece), block(z, piece), block(mine, srows)
    own = pltpu.make_async_copy(v_ref.at[:, mine_rows, :], v1.at[:, z_rows, :], own_sem)

    def zpeer(step):
        return (z + step) % nz

    def ppeer(step):
        other = (mine + step) % plane
        return z * 4 + other % 4, other // 4

    barrier = pltpu.get_barrier_semaphore()

    def greet_z(step, carry):
        pl.semaphore_signal(barrier, inc=1, device_id=(zpeer(step) * 4 + quad, col), device_id_type=MESH)
        return carry

    def greet_plane(step, carry):
        pl.semaphore_signal(barrier, inc=1, device_id=ppeer(step), device_id_type=MESH)
        return carry

    lax.fori_loop(1, nz, greet_z, 0)
    lax.fori_loop(1, plane, greet_plane, 0)
    load_v.wait()
    own.start()
    own.wait()
    pl.semaphore_wait(barrier, nz - 1 + plane - 1)

    turn = col + 4 * core

    def hop(index):
        return (index + turn) % nz

    def spread_one(held, which, index):
        part = held.at[z_rows, :]
        to = (z + hop(index)) % nz

        @pl.when(to != z)
        def _():
            send(part, part, g_send.at[which, 0], g1_recv.at[which, z], to * 4 + quad, col)

    def spread(held, which):
        def body(index, carry):
            spread_one(held, which, index)
            return carry

        lax.fori_loop(0, nz, body, 0)

    def hand_on(held, full, which, target):
        src = held.at[block(target, piece), :]
        dst = full.at[pl.ds(pl.multiple_of(quad * rows + col * piece, 8), piece), :]
        send(src, dst, g_send.at[which, 1], g2_recv.at[which, yl], z * 4 + (1 - yl) * 2 + core, target)

        @pl.when(target != col)
        def _():
            send(src, dst, g_send.at[which, 2], g2_recv.at[which, yl], row, target)

        @pl.when(target == col)
        def _():
            pltpu.make_async_copy(src, dst, g2_recv.at[which, yl]).start()

    def deliver(held, full, which, first, last, following=None):
        def body(index, carry):
            target = (z + nz - hop(index)) % nz

            @pl.when(target != z)
            def _():
                drain(held.at[block(target, piece), :], g1_recv.at[which, target])

            hand_on(held, full, which, target)
            if following is not None:
                spread_one(following, which + 1, index)
            return carry

        lax.fori_loop(first, last, body, 0)

    def relay(full, which):
        for side in range(2):
            part = full.at[block(side * 2 + core, rows), :]
            drain(part, g2_recv.at[which, side])
            send(part, part, g_send.at[which, 3 + side], g3_recv.at[which, side], z * 4 + yl * 2 + (1 - core), col)

    def partner(full, which, side):
        drain(full.at[block(side * 2 + (1 - core), rows), :], g3_recv.at[which, side])

    def settle(held, full, which):
        drain(held.at[0:(nz - 1) * piece, :], g_send.at[which, 0])
        drain(held.at[0:nz * piece, :], g_send.at[which, 1])
        drain(held.at[0:(nz - 1) * piece, :], g_send.at[which, 2])
        for side in range(2):
            drain(full.at[0:rows, :], g_send.at[which, 3 + side])

    def own_rows(group):
        return s_rows if group == 1 else block(mine // 2, srows)

    def if_owner(group):
        return pl.when(core == 0) if group != 1 else (lambda body: body())

    def sum_start(group):
        if group == 1:
            def body(step, carry):
                to_row, to_col = ppeer(step)
                other = (mine + step) % plane
                send(sp.at[group, block(other, srows), :], srs.at[group, mine], ss_send.at[group], ss_recv.at[group], to_row, to_col)
                return carry

            lax.fori_loop(1, plane, body, 0)
        else:
            def body(step, carry):
                owner = (mine // 2 + step) % (plane // 2)

                @pl.when((step > 0) | (core == 1))
                def _():
                    send(sp.at[group, block(owner, srows), :], srs.at[group, mine], ss_send.at[group], ss_recv.at[group], z * 4 + (owner % 2) * 2, owner // 2)

                return carry

            lax.fori_loop(0, plane // 2, body, 0)

        @if_owner(group)
        def _():
            srs[group, mine] = sp[group, own_rows(group), :]

    def sum_level(group):
        @if_owner(group)
        def _():
            drain(srs.at[group, 0:plane - 1], ss_recv.at[group])
            szs[group, z] = jnp.sum(srs[group], axis=0)

            def body(step, carry):
                part = szs.at[group, z]
                send(part, part, sz_send.at[group], sz_recv.at[group], zpeer(step) * 4 + quad, col)
                return carry

            lax.fori_loop(1, nz, body, 0)

    def sum_share(group):
        @if_owner(group)
        def _():
            drain(szs.at[group, 0:nz - 1], sz_recv.at[group])
            sf[group, own_rows(group), :] = jnp.sum(szs[group], axis=0)

            def body(step, carry):
                to_row, to_col = ppeer(step)
                part = sf.at[group, own_rows(group), :]
                send(part, part, sg_send.at[group], sg_recv.at[group], to_row, to_col)
                return carry

            lax.fori_loop(1, plane, body, 0)

    def drain_others(ref, sem):
        for parity in range(2):
            @pl.when(core == parity)
            def _(parity=parity):
                drain(ref.at[0:(plane // 2 - 1 + parity) * srows, :], sem)

    def sum_end(group):
        if group == 1:
            drain(sf.at[group, 0:(plane - 1) * srows, :], sg_recv.at[group])
        else:
            drain_others(sf.at[group], sg_recv.at[group])

    def sum_settle(group):
        if group == 1:
            drain(srs.at[group, 0:plane - 1], ss_send.at[group])
        else:
            drain_others(sf.at[group], ss_send.at[group])

        @if_owner(group)
        def _():
            drain(szs.at[group, 0:nz - 1], sz_send.at[group])
            drain(srs.at[group, 0:plane - 1], sg_send.at[group])

    spread(v1.at[0], 0)
    na, nb = v_ref[0, mine_rows, :], v_ref[1, mine_rows, :]
    sp[0, :size] = exact(na, nb, TN)
    sum_start(0)
    load.wait()
    ah[...], al[...] = halves(a_buf[...])
    deliver(v1.at[0], vc.at[0], 0, 0, nz, v1.at[1])
    deliver(v1.at[1], vc.at[1], 1, 0, nz // 2)
    relay(vc.at[0], 0)
    deliver(v1.at[1], vc.at[1], 1, nz // 2, nz)
    sum_level(0)

    rights = (right_a, right_b)

    def fold(full, panel, base, span):
        high, low = halves(full[span, :])
        rights[panel][span, base:base + size] = high
        rights[panel][span, base + size:base + 2 * size] = low

    for panel in range(2):
        if panel:
            relay(vc.at[1], 1)
            sum_share(0)
        held = rights[panel]
        for side in range(2):
            partner(vc.at[panel], panel, side)
        fold(vc.at[panel], panel, 2 * size, slice(0, width))
        both = lax.dot_general(ah[...], held[:, 2 * size:], NN, preferred_element_type=F32)
        part = lax.dot_general(al[...], held[:, 2 * size:3 * size], NN, preferred_element_type=F32)
        p_buf[panel] = part + both[:, size:] + both[:, :size]

        def scatter(step, carry, panel=panel):
            to = (col + step) % nz
            send(p_buf.at[panel, block(to, piece), :], rs.at[panel, mine_rows, :], rs_send.at[panel], rs_recv.at[panel], row, to)
            return carry

        lax.fori_loop(1, nz, scatter, 0)
        rs[panel, mine_rows, :] = p_buf[panel, mine_rows, :]

    xn = nz // 2
    facing = (col + xn) % nz

    def gather_send(panel, owner, with_facing):
        part = yr.at[panel, block(owner, piece), :]
        if with_facing:
            send(part, part, ag_send.at[panel], ap_recv.at[panel], row, facing)

        def body(step, carry):
            to = (col // xn) * xn + (col + step) % xn
            send(part, part, ag_send.at[panel], ag_recv.at[panel], row, to)
            return carry

        lax.fori_loop(1, xn, body, 0)

    def gather_pass(panel):
        drain(yr.at[panel, block(facing, piece), :], ap_recv.at[panel])
        gather_send(panel, facing, False)

    def gather_end(panel):
        if xn > 1:
            drain(yr.at[panel, 0:2 * (xn - 1) * piece, :], ag_recv.at[panel])

    def reduced(panel):
        drain(rs.at[panel, 0:(nz - 1) * piece, :], rs_recv.at[panel])
        total = rs[panel, 0:piece, :]
        for other in range(1, nz):
            total = total + rs[panel, other * piece:(other + 1) * piece, :]
        y1[panel, z_rows, :] = total
        yr[panel, mine_rows, :] = total
        spread(y1.at[panel], 2 + panel)
        sp[1 + panel, :size] = exact(nb if panel else na, total, TN)
        if panel == 0:
            sp[1, size:] = exact(nb, total, TN)
        sum_start(1 + panel)
        gather_send(panel, col, True)

    reduced(0)

    load_f.wait()
    f1, f2 = f_ref[0], f_ref[1]
    va, vb = v_ref[0], v_ref[1]
    sum_end(0)
    gram = sf[0, :size]
    e = exact(f1, exact(gram, f2))

    def keep(high_ref, low_ref, index, value):
        high, low = halves(value)
        high_ref[:, 2 * index * size:(2 * index + 1) * size] = high
        high_ref[:, (2 * index + 1) * size:(2 * index + 2) * size] = high
        low_ref[:, index * size:(index + 1) * size] = low

    keep(lh_a, ll_a, 0, exact(va, f1, NT) - exact(vb, e, NT))
    keep(lh_b, ll_b, 0, exact(vb, f2, NT))

    deliver(y1.at[0], yc.at[0], 2, 0, nz // 2)
    sum_level(1)
    reduced(1)
    deliver(y1.at[0], yc.at[0], 2, nz // 2, nz)
    gather_pass(0)
    sum_share(1)
    deliver(y1.at[1], yc.at[1], 3, 0, nz // 2)
    sum_level(2)
    deliver(y1.at[1], yc.at[1], 3, nz // 2, nz)
    relay(yc.at[0], 2)
    gather_end(0)
    ya = yr[0]
    most = exact(ya, f1)
    crossed = exact(ya, e)
    sum_share(2)
    gather_pass(1)
    for side in range(2):
        partner(yc.at[0], 2, side)
    fold(yc.at[0], 0, 0, slice(0, width))
    sum_end(1)
    s11, s21 = sf[1, :size], sf[1, size:]
    k1 = exact(exact(f1, s11, TN), f1)
    fs = exact(f1, s21, (((0,), (1,)), ((), ())))
    kg = exact(k1, gram)
    mixed = exact(kg - fs, f2)
    gt = exact(gram, fs - 0.5 * kg, TN)
    keep(lh_a, ll_a, 1, most - exact(va, k1) + exact(vb, mixed, NT))

    def first_terms(index, carry):
        span = pl.ds(pl.multiple_of(index * tile, tile), tile)
        a_buf[:, span] = a_buf[:, span] - drop(lh_a, ll_a, right_a, span)
        return carry

    for index in range(0, width, 256):
        span = slice(index, index + 256)
        a_buf[:, span] = a_buf[:, span] - drop(lh_a, ll_a, right_a, span)
    relay(yc.at[1], 3)
    gather_end(1)
    rest = exact(yr[1], f2) - crossed + exact(va, mixed)
    sum_end(2)
    k2 = exact(exact(f2, sf[2, :size] - gt - gt.T, TN), f2)
    keep(lh_b, ll_b, 1, rest - exact(vb, k2))

    for side in range(2):
        partner(yc.at[1], 3, side)
    fold(yc.at[1], 1, 0, slice(0, width))
    for panel in range(2):
        settle(v1.at[panel], vc.at[panel], panel)
        settle(y1.at[panel], yc.at[panel], 2 + panel)
        drain(rs.at[panel, 0:(nz - 1) * piece, :], rs_send.at[panel])
        drain(rs.at[panel, 0:(nz - 1) * piece, :], ag_send.at[panel])
    for group in range(3):
        sum_settle(group)


def apply_update(tile, a_ref, right, lh, ll, out, stage, sems):
    width = out.shape[1]
    ends = list(range(512, width, 512))
    stores = []
    for index, (start, stop) in enumerate(zip([0] + ends, ends + [width])):
        span = slice(start, stop)
        stage[:, span] = a_ref[:, span] - drop(lh, ll, right, span)
        stores.append(pltpu.make_async_copy(stage.at[:, span], out.at[:, span], sems.at[index]))
        stores[-1].start()
    for store in stores:
        store.wait()


def shards(nz, matrix, panels, factors):
    rows, width = matrix.shape
    size = panels.shape[2]
    srows = 2 * size // (4 * nz)
    tile = 896 if width % 896 == 0 else width
    vmem = pl.BlockSpec(memory_space=pltpu.VMEM)
    hbm = pl.BlockSpec(memory_space=pltpu.HBM)
    block = pltpu.VMEM((2, rows, size), F32)
    wide = pltpu.VMEM((2, width, size), F32)
    sums = pltpu.VMEM((3, 2 * size, size), F32)
    dma = pltpu.SemaphoreType.DMA
    held = pl.pallas_call(
        functools.partial(exchange, nz, tile),
        out_shape=(
            jax.ShapeDtypeStruct(matrix.shape, F32),
            jax.ShapeDtypeStruct((width, 4 * size), BF16),
            jax.ShapeDtypeStruct((rows, 4 * size), BF16),
            jax.ShapeDtypeStruct((rows, 2 * size), BF16),
        ),
        in_specs=[hbm, hbm, hbm],
        out_specs=(vmem,) * 4,
        scratch_shapes=[
            pltpu.VMEM((width, 4 * size), BF16), pltpu.VMEM((rows, 4 * size), BF16),
            pltpu.VMEM((rows, 2 * size), BF16),
            pltpu.VMEM((rows, width), BF16), pltpu.VMEM((rows, width), BF16),
            block, pltpu.VMEM(factors.shape, F32), wide, wide,
            block, block, block, block, block,
            sums, pltpu.VMEM((3, 4 * nz, srows, size), F32),
            pltpu.VMEM((3, nz, srows, size), F32), sums,
            dma(()), dma(()), dma(()), dma(()), dma((4, 5)), dma((4, nz)), dma((4, 2)), dma((4, 2)),
        ] + [dma((2,))] * 5 + [dma((3,))] * 6,
        compiler_params=pltpu.CompilerParams(collective_id=0, has_side_effects=True, vmem_limit_bytes=40 << 20),
        name="exchange",
    )(*(pltpu.with_memory_space_constraint(x, pltpu.HBM) for x in (matrix, panels, factors)))
    return pl.pallas_call(
        functools.partial(apply_update, tile),
        out_shape=jax.ShapeDtypeStruct(matrix.shape, F32),
        in_specs=[vmem] * 4,
        out_specs=hbm,
        scratch_shapes=[pltpu.VMEM((rows, width), F32), dma((8,))],
        compiler_params=pltpu.CompilerParams(vmem_limit_bytes=24 << 20),
        name="apply_update",
    )(*held)


def solution(mesh):
    placed = (P("row", "col"), P(None, "row", None), P())
    return jax.shard_map(
        functools.partial(shards, mesh.shape["col"]),
        mesh=mesh, in_specs=placed, out_specs=P("row", "col"), check_vma=False,
    )
```
